32 devices in a mesh: tm: 2 (over y), space: 16 (over z, x, core).
Axes of the slice: x: 2, y: 2, z: 4, core: 2. Of those that a mesh axis runs over, the one named last changes fastest.
Arguments:
- intensity: float32 [32, 128, 512], P('tm', 'space'), may hold values from 0.05 to 5
- w_first: bfloat16 [3, 3, 48, 32], replicated, may hold values from -0.5 to 0.5
- w_rest: bfloat16 [5, 3, 3, 48, 48], replicated, may hold values from -0.4375 to 0.4375
Outputs:
- front_maps: float32 [48, 128, 512], P(None, 'space', 'tm')
The draws below stay inside these ranges and needn't reach their ends.
All inputs are finite; a program needn't handle non-finite values.
Results may differ from the reference program's by a relative error of at most 0.03.
Values may be sent and summed in bfloat16 or wider, within the bound.
No kernel may reach another device: no remote copies, remote signals or barrier semaphores. Data moves between devices by JAX's collectives and lax.ppermute only.
A program may use at most 64 MiB of HBM per device.

```python
import math
import jax
import jax.numpy as jnp
from jax import lax

ACQUISITIONS = 32
CHANNELS = 48
LAYERS = 6
RADIUS = 3
GRID_COLS = 128
GRID_ROWS = 512


def block_scale(key, shape, split, least, top_value):
    def one(dim, blocks):
        steps = jax.random.uniform(jax.random.fold_in(jax.random.fold_in(key, 6), dim), (blocks,), jnp.float32, least / len(split), top_value / len(split))
        return jnp.repeat(jnp.exp(steps), shape[dim] // blocks).reshape((-1,) + (1,) * (len(shape) - dim - 1))

    level = one(*split[0])
    for cut in split[1:]:
        level = level * one(*cut)
    return level


def scatter_about(key, dims, deviation, most, kind=jnp.bfloat16):
    return jnp.clip(deviation * jax.random.normal(key, dims, jnp.float32), -most, most).astype(kind)


def setup_inputs(seed: int = 0) -> dict:
    arg_keys = jax.random.split(jax.random.key(seed), 4)
    return {
        "intensity": jnp.clip(jnp.exp(math.log(5.0) - 4.6051702 * jax.random.uniform(arg_keys[0], (ACQUISITIONS, GRID_COLS, GRID_ROWS), jnp.float32) ** block_scale(arg_keys[0], (ACQUISITIONS, GRID_COLS, GRID_ROWS), ((0, 2), (1, 16)), -0.2, 0.2)), 0.05, 5.0),
        "w_first": scatter_about(arg_keys[1], (3, 3, CHANNELS, ACQUISITIONS), (9 * ACQUISITIONS // 2) ** -0.5, 0.5),
        "w_rest": scatter_about(arg_keys[2], (LAYERS - 1, 3, 3, CHANNELS, CHANNELS), (9 * CHANNELS // 2) ** -0.5, 0.4375),
    }


def window_count(length):
    places = jnp.arange(length, dtype=jnp.int32)
    upper = jnp.minimum(places + RADIUS, length - 1)
    lower = jnp.maximum(places - RADIUS, 0)
    return (upper - lower + 1).astype(jnp.float32)


def conv_full(activation, kernel):
    inputs = activation.astype(jnp.float32)[None]
    filters = jnp.transpose(kernel, (2, 3, 0, 1)).astype(jnp.float32)
    result = lax.conv_general_dilated(inputs, filters, (1, 1), ((1, 1), (1, 1)), dimension_numbers=("NCHW", "OIHW", "NCHW"), precision=lax.Precision.HIGHEST)
    return result[0]


def reference(intensity, w_first, w_rest):
    widened = jnp.pad(intensity, ((0, 0), (RADIUS, RADIUS), (RADIUS, RADIUS)))
    col_sum = widened[:, 0:GRID_COLS, :]
    for k in range(1, 2 * RADIUS + 1):
        col_sum = col_sum + widened[:, k:k + GRID_COLS, :]
    box_sum = col_sum[:, :, 0:GRID_ROWS]
    for k in range(1, 2 * RADIUS + 1):
        box_sum = box_sum + col_sum[:, :, k:k + GRID_ROWS]
    cell_count = window_count(GRID_COLS)[:, None] * window_count(GRID_ROWS)[None, :]
    local_mean = box_sum / cell_count
    log_mean = jnp.log(local_mean)
    ratio_sum = jnp.sum(intensity / local_mean, axis=0)
    features = (log_mean + jnp.log(ratio_sum / ACQUISITIONS)[None]).astype(jnp.bfloat16)
    activation = jnp.maximum(conv_full(features, w_first), 0.0).astype(jnp.bfloat16)
    result = None
    for depth_index in range(LAYERS - 1):
        summed = conv_full(activation, w_rest[depth_index])
        if depth_index < LAYERS - 2:
            activation = jnp.maximum(summed, 0.0).astype(jnp.bfloat16)
        else:
            result = summed
    return result
```

```python
import jax
import jax.numpy as jnp
from jax import lax
from jax.experimental import pallas as pl
from jax.experimental.pallas import tpu as pltpu
from jax.sharding import PartitionSpec as P

LAYERS = 6
RADIUS = 3
HALO = RADIUS + LAYERS
MARGIN = 16
LANES = 128


def shifted(x, axis, by):
    size = lax.axis_size(axis)
    pairs = [(i, i + by) for i in range(size) if 0 <= i + by < size]
    return lax.ppermute(x, axis, pairs)


def window_rows(tile, rows):
    return min(rows, tile + LANES * (1 if rows <= 2 * tile else 2))


def window_base(index, tile, rows):
    return jnp.clip(index * tile - LANES, 0, rows - window_rows(tile, rows))


def rolled(x, by):
    return pltpu.roll(x, by % x.shape[-1], x.ndim - 1)


def body(place, far_lo, lo, own, hi, far_hi, w1, wr, out, inten, sums, act_a, act_b):
    acqs, width = own.shape[1:]
    cols = own.shape[0]
    tile = out.shape[2]
    channels = out.shape[0]
    first_col, all_cols = place[0], place[1]
    base, all_rows, offset = place[2], place[3], place[4]

    lane = lax.broadcasted_iota(jnp.int32, (1, width), 1)
    inside = (lane >= offset - MARGIN) & (lane < offset + tile + MARGIN)
    row_mask = inside.astype(jnp.float32)

    pieces = [(far_lo, 0, HALO - cols), (lo, 0, cols), (own, 0, cols), (hi, 0, cols), (far_hi, 0, HALO - cols)]
    at = 0
    for ref, start, count in pieces:
        for k in range(count):
            inten[at] = jnp.where(inside, jnp.exp(ref[start + k].astype(jnp.float32)), 0.0)
            at += 1

    feature_cols = cols + 2 * LAYERS
    for c in range(at):
        g = first_col - HALO + c
        if c < HALO or c >= HALO + cols:
            ok = ((g >= 0) & (g < all_cols)).astype(jnp.float32)
            inten[c] = inten[c] * ok

    row = base + lane
    row_count = jnp.minimum(row + RADIUS, all_rows - 1) - jnp.maximum(row - RADIUS, 0) + 1
    row_count = row_count.astype(jnp.float32)

    def despeckle(f, _):
        total = inten[f]
        for k in range(1, 2 * RADIUS + 1):
            total = total + inten[f + k]
        three = rolled(total, 1) + total + rolled(total, -1)
        box = rolled(three, 2) + total + rolled(three, -2)
        g = first_col - LAYERS + f
        col_count = jnp.minimum(g + RADIUS, all_cols - 1) - jnp.maximum(g - RADIUS, 0) + 1
        col_count = jnp.maximum(col_count, 1).astype(jnp.float32)
        local_mean = box / (row_count * col_count)
        ratio = jnp.sum(inten[f + RADIUS] / local_mean, axis=0, keepdims=True)
        feature = jnp.log(local_mean) + jnp.log(ratio / acqs)
        ok = (g >= 0) & (g < all_cols)
        feature = jnp.where(inside & ok, feature, 0.0)
        at = pl.multiple_of(f * 3 * acqs, 16)
        act_a[pl.ds(at, acqs), :] = rolled(feature, 1).astype(jnp.bfloat16)
        act_a[pl.ds(at + acqs, acqs), :] = feature.astype(jnp.bfloat16)
        act_a[pl.ds(at + 2 * acqs, acqs), :] = rolled(feature, -1).astype(jnp.bfloat16)
        return 0

    lax.fori_loop(0, feature_cols, despeckle, 0)

    source, target = act_a, act_b
    depth = acqs
    for layer in range(LAYERS):
        weight = w1[...] if layer == 0 else wr[layer - 1]
        out_cols = feature_cols - 2 * (layer + 1)
        last = layer == LAYERS - 1

        def column(j, _, source=source, target=target, depth=depth, weight=weight, layer=layer, last=last):
            at = pl.multiple_of(j * 3 * depth, 16)
            summed = jnp.dot(weight, source[pl.ds(at, 9 * depth), :], preferred_element_type=jnp.float32)
            g = first_col - (LAYERS - 1 - layer) + j
            ok = ((g >= 0) & (g < all_cols)).astype(jnp.float32)
            hidden = jnp.maximum(summed, 0.0) * (row_mask * ok)
            to = pl.multiple_of(j * 3 * channels, 16)
            target[pl.ds(to, channels), :] = rolled(hidden, 1).astype(jnp.bfloat16)
            target[pl.ds(to + channels, channels), :] = hidden.astype(jnp.bfloat16)
            target[pl.ds(to + 2 * channels, channels), :] = rolled(hidden, -1).astype(jnp.bfloat16)
            return 0

        if not last:
            lax.fori_loop(0, out_cols, column, 0)
        else:
            lanes = pl.ds(pl.multiple_of(offset, LANES), tile)
            for j in range(out_cols):
                out[:, j, :] = jnp.dot(
                    weight,
                    source[j * 3 * depth : (j * 3 + 9) * depth, lanes],
                    preferred_element_type=jnp.float32,
                )
        source, target = target, source
        depth = channels


def shards(intensity, w_first, w_rest):
    acqs_own, cols, rows = intensity.shape
    tm = lax.axis_size("tm")
    space = lax.axis_size("space")
    m = lax.axis_index("tm")
    s = lax.axis_index("space")
    tile = rows // tm
    width = window_rows(tile, rows)
    channels, acqs = w_first.shape[2:]

    coded = jnp.log(intensity).astype(jnp.bfloat16).transpose(1, 0, 2)
    base = window_base(m, tile, rows)
    parts = [lax.dynamic_slice_in_dim(coded, base, width, axis=2)]
    for d in range(1, tm):
        to = window_base((m + d) % tm, tile, rows)
        piece = lax.dynamic_slice_in_dim(coded, to, width, axis=2)
        parts.append(lax.ppermute(piece, "tm", [(i, (i + d) % tm) for i in range(tm)]))
    own = jnp.concatenate(parts, axis=1)
    order = (m - jnp.arange(tm)) % tm
    w1 = jnp.take(w_first.reshape(3, 3, channels, tm, acqs_own), order, axis=3)
    w1 = w1.reshape(3, 3, channels, acqs).transpose(2, 0, 1, 3).reshape(channels, 9 * acqs)
    wr = w_rest.transpose(0, 3, 1, 2, 4).reshape(LAYERS - 1, channels, 9 * channels)

    far = HALO - cols
    far_lo = shifted(own[cols - far :], "space", 2)
    far_hi = shifted(own[:far], "space", -2)
    lo = shifted(own, "space", 1)
    hi = shifted(own, "space", -1)

    place = jnp.stack(
        [s * cols, jnp.int32(cols * space), base, jnp.int32(rows), m * tile - base]
    ).astype(jnp.int32)
    vmem = pl.BlockSpec(memory_space=pltpu.VMEM)
    feature_cols = cols + 2 * LAYERS
    act = (feature_cols * 3 * channels, width)
    return pl.pallas_call(
        body,
        out_shape=jax.ShapeDtypeStruct((channels, cols, tile), jnp.float32),
        in_specs=[pl.BlockSpec(memory_space=pltpu.SMEM)] + [vmem] * 7,
        out_specs=vmem,
        scratch_shapes=[
            pltpu.VMEM((cols + 2 * HALO, acqs, width), jnp.float32),
            pltpu.VMEM((8, 128), jnp.float32),
            pltpu.VMEM(act, jnp.bfloat16),
            pltpu.VMEM(act, jnp.bfloat16),
        ],
        compiler_params=pltpu.CompilerParams(vmem_limit_bytes=40 * 1024 * 1024),
    )(place, far_lo, lo, own, hi, far_hi, w1, wr)


def solution(mesh):
    in_specs = (P("tm", "space", None), P(), P())
    out_specs = P(None, "space", "tm")
    return jax.shard_map(shards, mesh=mesh, in_specs=in_specs, out_specs=out_specs, check_vma=False)
```

```python
import jax
import jax.numpy as jnp
from jax import lax
from jax.experimental import pallas as pl
from jax.experimental.pallas import tpu as pltpu
from jax.sharding import PartitionSpec as P

LAYERS = 6
RADIUS = 3
HALO = RADIUS + LAYERS
MARGIN = 16
LANES = 128


def shifted(x, axis, by):
    size = lax.axis_size(axis)
    pairs = [(i, i + by) for i in range(size) if 0 <= i + by < size]
    return lax.ppermute(x, axis, pairs)


def window_rows(tile, rows):
    return min(rows, tile + LANES * (1 if rows <= 2 * tile else 2))


def window_base(index, tile, rows):
    return jnp.clip(index * tile - LANES, 0, rows - window_rows(tile, rows))


def rolled(x, by):
    return pltpu.roll(x, by % x.shape[-1], x.ndim - 1)


def body(place, far_lo, lo, own, hi, far_hi, w1, wr, out, inten, act_a, act_b):
    acqs, width = own.shape[1:]
    cols = own.shape[0]
    tile = out.shape[2]
    channels = out.shape[0]
    first_col, all_cols = place[0], place[1]
    base, all_rows, offset = place[2], place[3], place[4]

    lane = lax.broadcasted_iota(jnp.int32, (1, width), 1)
    inside = (lane >= offset - MARGIN) & (lane < offset + tile + MARGIN)
    row_mask = inside.astype(jnp.float32)

    pieces = [(far_lo, 0, HALO - cols), (lo, 0, cols), (own, 0, cols), (hi, 0, cols), (far_hi, 0, HALO - cols)]
    at = 0
    for ref, start, count in pieces:
        for k in range(count):
            inten[at] = jnp.where(inside, jnp.exp(ref[start + k].astype(jnp.float32)), 0.0)
            at += 1

    feature_cols = cols + 2 * LAYERS
    for c in range(at):
        g = first_col - HALO + c
        if c < HALO or c >= HALO + cols:
            ok = ((g >= 0) & (g < all_cols)).astype(jnp.float32)
            inten[c] = inten[c] * ok

    row = base + lane
    row_count = jnp.minimum(row + RADIUS, all_rows - 1) - jnp.maximum(row - RADIUS, 0) + 1
    row_count = row_count.astype(jnp.float32)

    def despeckle(f, _):
        total = inten[f]
        for k in range(1, 2 * RADIUS + 1):
            total = total + inten[f + k]
        three = rolled(total, 1) + total + rolled(total, -1)
        box = rolled(three, 2) + total + rolled(three, -2)
        g = first_col - LAYERS + f
        col_count = jnp.minimum(g + RADIUS, all_cols - 1) - jnp.maximum(g - RADIUS, 0) + 1
        col_count = jnp.maximum(col_count, 1).astype(jnp.float32)
        local_mean = box / (row_count * col_count)
        ratio = jnp.sum(inten[f + RADIUS] / local_mean, axis=0, keepdims=True)
        feature = jnp.log(local_mean) + jnp.log(ratio / acqs)
        ok = (g >= 0) & (g < all_cols)
        feature = jnp.where(inside & ok, feature, 0.0)
        at = pl.multiple_of(f * 3 * acqs, 16)
        act_a[pl.ds(at, acqs), :] = rolled(feature, 1).astype(jnp.bfloat16)
        act_a[pl.ds(at + acqs, acqs), :] = feature.astype(jnp.bfloat16)
        act_a[pl.ds(at + 2 * acqs, acqs), :] = rolled(feature, -1).astype(jnp.bfloat16)
        return 0

    lax.fori_loop(0, feature_cols, despeckle, 0, unroll=4)

    source, target = act_a, act_b
    depth = acqs
    for layer in range(LAYERS):
        weight = w1[...] if layer == 0 else wr[layer - 1]
        out_cols = feature_cols - 2 * (layer + 1)
        last = layer == LAYERS - 1

        def column(j, source=source, target=target, depth=depth, weight=weight, layer=layer, last=last):
            at = j * 3 * depth
            summed = jnp.dot(weight, source[pl.ds(at, 9 * depth), :], preferred_element_type=jnp.float32)
            g = first_col - (LAYERS - 1 - layer) + j
            ok = ((g >= 0) & (g < all_cols)).astype(jnp.float32)
            hidden = jnp.maximum(summed, 0.0) * (row_mask * ok)
            to = j * 3 * channels
            target[pl.ds(to, channels), :] = rolled(hidden, 1).astype(jnp.bfloat16)
            target[pl.ds(to + channels, channels), :] = hidden.astype(jnp.bfloat16)
            target[pl.ds(to + 2 * channels, channels), :] = rolled(hidden, -1).astype(jnp.bfloat16)

        if not last:
            for j in range(out_cols):
                column(j)
        else:
            lanes = pl.ds(pl.multiple_of(offset, LANES), tile)
            for j in range(out_cols):
                out[:, j, :] = jnp.dot(
                    weight,
                    source[j * 3 * depth : (j * 3 + 9) * depth, lanes],
                    preferred_element_type=jnp.float32,
                )
        source, target = target, source
        depth = channels


def shards(intensity, w_first, w_rest):
    acqs_own, cols, rows = intensity.shape
    tm = lax.axis_size("tm")
    space = lax.axis_size("space")
    m = lax.axis_index("tm")
    s = lax.axis_index("space")
    tile = rows // tm
    width = window_rows(tile, rows)
    channels, acqs = w_first.shape[2:]

    coded = jnp.log(intensity).astype(jnp.bfloat16).transpose(1, 0, 2)
    base = window_base(m, tile, rows)
    parts = [lax.dynamic_slice_in_dim(coded, base, width, axis=2)]
    for d in range(1, tm):
        to = window_base((m + d) % tm, tile, rows)
        piece = lax.dynamic_slice_in_dim(coded, to, width, axis=2)
        parts.append(lax.ppermute(piece, "tm", [(i, (i + d) % tm) for i in range(tm)]))
    own = jnp.concatenate(parts, axis=1)
    order = (m - jnp.arange(tm)) % tm
    w1 = jnp.take(w_first.reshape(3, 3, channels, tm, acqs_own), order, axis=3)
    w1 = w1.reshape(3, 3, channels, acqs).transpose(2, 0, 1, 3).reshape(channels, 9 * acqs)
    wr = w_rest.transpose(0, 3, 1, 2, 4).reshape(LAYERS - 1, channels, 9 * channels)

    far = HALO - cols
    own, first, final = lax.optimization_barrier((own, own[:far], own[cols - far :]))
    far_lo = shifted(final, "space", 2)
    far_hi = shifted(first, "space", -2)
    lo = shifted(own, "space", 1)
    hi = shifted(own, "space", -1)

    place = jnp.stack(
        [s * cols, jnp.int32(cols * space), base, jnp.int32(rows), m * tile - base]
    ).astype(jnp.int32)
    vmem = pl.BlockSpec(memory_space=pltpu.VMEM)
    feature_cols = cols + 2 * LAYERS
    act = (feature_cols * 3 * channels, width)
    return pl.pallas_call(
        body,
        out_shape=jax.ShapeDtypeStruct((channels, cols, tile), jnp.float32),
        in_specs=[pl.BlockSpec(memory_space=pltpu.SMEM)] + [vmem] * 7,
        out_specs=vmem,
        scratch_shapes=[
            pltpu.VMEM((cols + 2 * HALO, acqs, width), jnp.float32),
            pltpu.VMEM(act, jnp.bfloat16),
            pltpu.VMEM(act, jnp.bfloat16),
        ],
        compiler_params=pltpu.CompilerParams(vmem_limit_bytes=40 * 1024 * 1024),
    )(place, far_lo, lo, own, hi, far_hi, w1, wr)


def solution(mesh):
    in_specs = (P("tm", "space", None), P(), P())
    out_specs = P(None, "space", "tm")
    return jax.shard_map(shards, mesh=mesh, in_specs=in_specs, out_specs=out_specs, check_vma=False)
```

```python
import jax
import jax.numpy as jnp
from jax import lax
from jax.experimental import pallas as pl
from jax.experimental.pallas import tpu as pltpu
from jax.sharding import PartitionSpec as P

LAYERS = 6
RADIUS = 3
HALO = RADIUS + LAYERS
MARGIN = 16
LANES = 128


def shifted(x, axis, by):
    size = lax.axis_size(axis)
    pairs = [(i, i + by) for i in range(size) if 0 <= i + by < size]
    return lax.ppermute(x, axis, pairs)


def window_rows(tile, rows):
    return min(rows, tile + LANES * (1 if rows <= 2 * tile else 2))


def window_base(index, tile, rows):
    return jnp.clip(index * tile - LANES, 0, rows - window_rows(tile, rows))


def rolled(x, by):
    return pltpu.roll(x, by % x.shape[-1], x.ndim - 1)


def body(place, far, lo, own, hi, w1, wr, out, inten, act_a, act_b):
    acqs, width = own.shape[1:]
    cols = own.shape[0]
    tile = out.shape[2]
    channels = out.shape[0]
    first_col, all_cols = place[0], place[1]
    base, all_rows, offset = place[2], place[3], place[4]

    lane = lax.broadcasted_iota(jnp.int32, (1, width), 1)
    inside = (lane >= offset - MARGIN) & (lane < offset + tile + MARGIN)
    row_mask = inside.astype(jnp.float32)

    more = HALO - cols
    pieces = [(far, 0, more), (lo, 0, cols), (own, 0, cols), (hi, 0, cols), (far, more, more)]
    at = 0
    for ref, start, count in pieces:
        for k in range(count):
            inten[at] = jnp.where(inside, jnp.exp(ref[start + k].astype(jnp.float32)), 0.0)
            at += 1

    feature_cols = cols + 2 * LAYERS
    for c in range(at):
        g = first_col - HALO + c
        if c < HALO or c >= HALO + cols:
            ok = ((g >= 0) & (g < all_cols)).astype(jnp.float32)
            inten[c] = inten[c] * ok

    row = base + lane
    row_count = jnp.minimum(row + RADIUS, all_rows - 1) - jnp.maximum(row - RADIUS, 0) + 1
    row_count = row_count.astype(jnp.float32)

    def despeckle(f, _):
        total = inten[f]
        for k in range(1, 2 * RADIUS + 1):
            total = total + inten[f + k]
        three = rolled(total, 1) + total + rolled(total, -1)
        box = rolled(three, 2) + total + rolled(three, -2)
        g = first_col - LAYERS + f
        col_count = jnp.minimum(g + RADIUS, all_cols - 1) - jnp.maximum(g - RADIUS, 0) + 1
        col_count = jnp.maximum(col_count, 1).astype(jnp.float32)
        local_mean = box / (row_count * col_count)
        ratio = jnp.sum(inten[f + RADIUS] / local_mean, axis=0, keepdims=True)
        feature = jnp.log(local_mean) + jnp.log(ratio / acqs)
        ok = (g >= 0) & (g < all_cols)
        feature = jnp.where(inside & ok, feature, 0.0)
        at = pl.multiple_of(f * 3 * acqs, 16)
        act_a[pl.ds(at, acqs), :] = rolled(feature, 1).astype(jnp.bfloat16)
        act_a[pl.ds(at + acqs, acqs), :] = feature.astype(jnp.bfloat16)
        act_a[pl.ds(at + 2 * acqs, acqs), :] = rolled(feature, -1).astype(jnp.bfloat16)
        return 0

    lax.fori_loop(0, feature_cols, despeckle, 0, unroll=4)

    source, target = act_a, act_b
    depth = acqs
    for layer in range(LAYERS):
        weight = w1[...] if layer == 0 else wr[layer - 1]
        out_cols = feature_cols - 2 * (layer + 1)
        last = layer == LAYERS - 1

        def column(j, source=source, target=target, depth=depth, weight=weight, layer=layer, last=last):
            at = j * 3 * depth
            summed = jnp.dot(weight, source[pl.ds(at, 9 * depth), :], preferred_element_type=jnp.float32)
            g = first_col - (LAYERS - 1 - layer) + j
            ok = ((g >= 0) & (g < all_cols)).astype(jnp.float32)
            hidden = jnp.maximum(summed, 0.0) * (row_mask * ok)
            to = j * 3 * channels
            target[pl.ds(to, channels), :] = rolled(hidden, 1).astype(jnp.bfloat16)
            target[pl.ds(to + channels, channels), :] = hidden.astype(jnp.bfloat16)
            target[pl.ds(to + 2 * channels, channels), :] = rolled(hidden, -1).astype(jnp.bfloat16)

        if not last:
            for j in range(out_cols):
                column(j)
        else:
            lanes = pl.ds(pl.multiple_of(offset, LANES), tile)
            for j in range(out_cols):
                out[:, j, :] = jnp.dot(
                    weight,
                    source[j * 3 * depth : (j * 3 + 9) * depth, lanes],
                    preferred_element_type=jnp.float32,
                )
        source, target = target, source
        depth = channels


def shards(intensity, w_first, w_rest):
    acqs_own, cols, rows = intensity.shape
    tm = lax.axis_size("tm")
    space = lax.axis_size("space")
    m = lax.axis_index("tm")
    s = lax.axis_index("space")
    tile = rows // tm
    width = window_rows(tile, rows)
    channels, acqs = w_first.shape[2:]

    coded = jnp.log(intensity).astype(jnp.bfloat16).transpose(1, 0, 2)
    base = window_base(m, tile, rows)

    def gathered(x):
        parts = [lax.dynamic_slice_in_dim(x, base, width, axis=2)]
        for d in range(1, tm):
            to = window_base((m + d) % tm, tile, rows)
            piece = lax.dynamic_slice_in_dim(x, to, width, axis=2)
            parts.append(lax.ppermute(piece, "tm", [(i, (i + d) % tm) for i in range(tm)]))
        return jnp.concatenate(parts, axis=1)

    far = HALO - cols
    own = gathered(coded)
    far_own = jnp.concatenate(
        [shifted(coded[cols - far :], "space", 2), shifted(coded[:far], "space", -2)], axis=0
    )
    far_cols = gathered(far_own)
    lo = shifted(own, "space", 1)
    hi = shifted(own, "space", -1)

    order = (m - jnp.arange(tm)) % tm
    w1 = jnp.take(w_first.reshape(3, 3, channels, tm, acqs_own), order, axis=3)
    w1 = w1.reshape(3, 3, channels, acqs).transpose(2, 0, 1, 3).reshape(channels, 9 * acqs)
    wr = w_rest.transpose(0, 3, 1, 2, 4).reshape(LAYERS - 1, channels, 9 * channels)

    place = jnp.stack(
        [s * cols, jnp.int32(cols * space), base, jnp.int32(rows), m * tile - base]
    ).astype(jnp.int32)
    vmem = pl.BlockSpec(memory_space=pltpu.VMEM)
    feature_cols = cols + 2 * LAYERS
    act = (feature_cols * 3 * channels, width)
    return pl.pallas_call(
        body,
        out_shape=jax.ShapeDtypeStruct((channels, cols, tile), jnp.float32),
        in_specs=[pl.BlockSpec(memory_space=pltpu.SMEM)] + [vmem] * 6,
        out_specs=vmem,
        scratch_shapes=[
            pltpu.VMEM((cols + 2 * HALO, acqs, width), jnp.float32),
            pltpu.VMEM(act, jnp.bfloat16),
            pltpu.VMEM(act, jnp.bfloat16),
        ],
        compiler_params=pltpu.CompilerParams(vmem_limit_bytes=40 * 1024 * 1024),
    )(place, far_cols, lo, own, hi, w1, wr)


def solution(mesh):
    in_specs = (P("tm", "space", None), P(), P())
    out_specs = P(None, "space", "tm")
    return jax.shard_map(shards, mesh=mesh, in_specs=in_specs, out_specs=out_specs, check_vma=False)
```

```python
import jax
import jax.numpy as jnp
from jax import lax
from jax.experimental import pallas as pl
from jax.experimental.pallas import tpu as pltpu
from jax.sharding import PartitionSpec as P

LAYERS = 6
RADIUS = 3
HALO = RADIUS + LAYERS
MARGIN = 16
LANES = 128


def paired(x, by, phase):
    size, groups = lax.axis_size("space"), lax.axis_size("tm")
    low = [i for i in range(size - by) if (i // by) % 2 == phase]
    partner = {i: i + by for i in low} | {i + by: i for i in low}
    alone = [i for i in range(size) if i not in partner]
    pairs = [(g * size + i, g * size + j) for g in range(groups) for i, j in partner.items()]
    if groups % 2 == 0:
        pairs += [(g * size + i, (g ^ 1) * size + i) for g in range(groups) for i in alone]
    else:
        pairs += [
            (g * size + i, g * size + j) for g in range(groups) for i, j in zip(alone, reversed(alone))
        ]
    return lax.ppermute(x, ("tm", "space"), pairs)


def window_rows(tile, rows):
    return min(rows, tile + LANES * (1 if rows <= 2 * tile else 2))


def window_base(index, tile, rows):
    return jnp.clip(index * tile - LANES, 0, rows - window_rows(tile, rows))


def rolled(x, by):
    return pltpu.roll(x, by % x.shape[-1], x.ndim - 1)


def body(place, far_in, far_out, own, mate, next_to, w1, wr, out, inten, act_a, act_b):
    acqs, width = own.shape[1:]
    cols = own.shape[0]
    tile = out.shape[2]
    channels = out.shape[0]
    first_col, all_cols = place[0], place[1]
    base, all_rows, offset = place[2], place[3], place[4]

    lane = lax.broadcasted_iota(jnp.int32, (1, width), 1)
    inside = (lane >= offset - MARGIN) & (lane < offset + tile + MARGIN)
    row_mask = inside.astype(jnp.float32)

    odd, odd_pair = place[5] == 1, place[6] == 1
    more = HALO - cols
    pieces = [(far_out, far_in, odd_pair, more), (next_to, mate, odd, cols), (own, own, None, cols)]
    pieces += [(mate, next_to, odd, cols), (far_in, far_out, odd_pair, more)]
    at = 0
    for ref, other, use_other, count in pieces:
        for k in range(count):
            coded = ref[k].astype(jnp.float32)
            if use_other is not None:
                coded = jnp.where(use_other, other[k].astype(jnp.float32), coded)
            inten[at] = jnp.where(inside, jnp.exp(coded), 0.0)
            at += 1

    feature_cols = cols + 2 * LAYERS
    for c in range(at):
        g = first_col - HALO + c
        if c < HALO or c >= HALO + cols:
            ok = ((g >= 0) & (g < all_cols)).astype(jnp.float32)
            inten[c] = inten[c] * ok

    row = base + lane
    row_count = jnp.minimum(row + RADIUS, all_rows - 1) - jnp.maximum(row - RADIUS, 0) + 1
    row_count = row_count.astype(jnp.float32)

    def despeckle(f, _):
        total = inten[f]
        for k in range(1, 2 * RADIUS + 1):
            total = total + inten[f + k]
        three = rolled(total, 1) + total + rolled(total, -1)
        box = rolled(three, 2) + total + rolled(three, -2)
        g = first_col - LAYERS + f
        col_count = jnp.minimum(g + RADIUS, all_cols - 1) - jnp.maximum(g - RADIUS, 0) + 1
        col_count = jnp.maximum(col_count, 1).astype(jnp.float32)
        local_mean = box / (row_count * col_count)
        ratio = jnp.sum(inten[f + RADIUS] / local_mean, axis=0, keepdims=True)
        feature = jnp.log(local_mean) + jnp.log(ratio / acqs)
        ok = (g >= 0) & (g < all_cols)
        feature = jnp.where(inside & ok, feature, 0.0)
        at = pl.multiple_of(f * 3 * acqs, 16)
        act_a[pl.ds(at, acqs), :] = rolled(feature, 1).astype(jnp.bfloat16)
        act_a[pl.ds(at + acqs, acqs), :] = feature.astype(jnp.bfloat16)
        act_a[pl.ds(at + 2 * acqs, acqs), :] = rolled(feature, -1).astype(jnp.bfloat16)
        return 0

    lax.fori_loop(0, feature_cols, despeckle, 0, unroll=4)

    source, target = act_a, act_b
    depth = acqs
    for layer in range(LAYERS):
        weight = w1[...] if layer == 0 else wr[layer - 1]
        out_cols = feature_cols - 2 * (layer + 1)
        last = layer == LAYERS - 1

        def column(j, source=source, target=target, depth=depth, weight=weight, layer=layer, last=last):
            at = j * 3 * depth
            summed = jnp.dot(weight, source[pl.ds(at, 9 * depth), :], preferred_element_type=jnp.float32)
            g = first_col - (LAYERS - 1 - layer) + j
            ok = ((g >= 0) & (g < all_cols)).astype(jnp.float32)
            hidden = jnp.maximum(summed, 0.0) * (row_mask * ok)
            to = j * 3 * channels
            target[pl.ds(to, channels), :] = rolled(hidden, 1).astype(jnp.bfloat16)
            target[pl.ds(to + channels, channels), :] = hidden.astype(jnp.bfloat16)
            target[pl.ds(to + 2 * channels, channels), :] = rolled(hidden, -1).astype(jnp.bfloat16)

        if not last:
            for j in range(out_cols):
                column(j)
        else:
            lanes = pl.ds(pl.multiple_of(offset, LANES), tile)
            for j in range(out_cols):
                out[:, j, :] = jnp.dot(
                    weight,
                    source[j * 3 * depth : (j * 3 + 9) * depth, lanes],
                    preferred_element_type=jnp.float32,
                )
        source, target = target, source
        depth = channels


def shards(intensity, w_first, w_rest):
    acqs_own, cols, rows = intensity.shape
    tm = lax.axis_size("tm")
    space = lax.axis_size("space")
    m = lax.axis_index("tm")
    s = lax.axis_index("space")
    tile = rows // tm
    width = window_rows(tile, rows)
    channels, acqs = w_first.shape[2:]

    coded = jnp.log(intensity).astype(jnp.bfloat16).transpose(1, 0, 2)
    base = window_base(m, tile, rows)
    parts = [lax.dynamic_slice_in_dim(coded, base, width, axis=2)]
    for d in range(1, tm):
        to = window_base((m + d) % tm, tile, rows)
        piece = lax.dynamic_slice_in_dim(coded, to, width, axis=2)
        parts.append(lax.ppermute(piece, "tm", [(i, (i + d) % tm) for i in range(tm)]))
    own = jnp.concatenate(parts, axis=1)
    order = (m - jnp.arange(tm)) % tm
    w1 = jnp.take(w_first.reshape(3, 3, channels, tm, acqs_own), order, axis=3)
    w1 = w1.reshape(3, 3, channels, acqs).transpose(2, 0, 1, 3).reshape(channels, 9 * acqs)
    wr = w_rest.transpose(0, 3, 1, 2, 4).reshape(LAYERS - 1, channels, 9 * channels)

    far = HALO - cols
    head, tail = own[:far], own[cols - far :]
    low = (s // 2) % 2 == 0
    inner, outer = jnp.where(low, tail, head), jnp.where(low, head, tail)
    own, inner, outer = lax.optimization_barrier((own, inner, outer))
    far_in = paired(inner, 2, 0)
    far_out = paired(outer, 2, 1)
    mate = paired(own, 1, 0)
    next_to = paired(own, 1, 1)

    place = jnp.stack(
        [s * cols, jnp.int32(cols * space), base, jnp.int32(rows), m * tile - base, s % 2, (s // 2) % 2]
    ).astype(jnp.int32)
    vmem = pl.BlockSpec(memory_space=pltpu.VMEM)
    feature_cols = cols + 2 * LAYERS
    act = (feature_cols * 3 * channels, width)
    return pl.pallas_call(
        body,
        out_shape=jax.ShapeDtypeStruct((channels, cols, tile), jnp.float32),
        in_specs=[pl.BlockSpec(memory_space=pltpu.SMEM)] + [vmem] * 7,
        out_specs=vmem,
        scratch_shapes=[
            pltpu.VMEM((cols + 2 * HALO, acqs, width), jnp.float32),
            pltpu.VMEM(act, jnp.bfloat16),
            pltpu.VMEM(act, jnp.bfloat16),
        ],
        compiler_params=pltpu.CompilerParams(vmem_limit_bytes=40 * 1024 * 1024),
    )(place, far_in, far_out, own, mate, next_to, w1, wr)


def solution(mesh):
    in_specs = (P("tm", "space", None), P(), P())
    out_specs = P(None, "space", "tm")
    return jax.shard_map(shards, mesh=mesh, in_specs=in_specs, out_specs=out_specs, check_vma=False)
```

```python
import jax
import jax.numpy as jnp
from jax import lax
from jax.experimental import pallas as pl
from jax.experimental.pallas import tpu as pltpu
from jax.sharding import PartitionSpec as P

LAYERS = 6
RADIUS = 3
HALO = RADIUS + LAYERS
MARGIN = 16
LANES = 128
PAIR = 2
BESIDE = 2


def swapped(x, lows, by):
    size, groups = lax.axis_size("space"), lax.axis_size("tm")
    partner = {i: i + by for i in lows} | {i + by: i for i in lows}
    alone = [i for i in range(size) if i not in partner]
    pairs = [(g * size + i, g * size + j) for g in range(groups) for i, j in partner.items()]
    if groups % 2 == 0:
        pairs += [(g * size + i, (g ^ 1) * size + i) for g in range(groups) for i in alone]
    else:
        pairs += [
            (g * size + i, g * size + j) for g in range(groups) for i, j in zip(alone, reversed(alone))
        ]
    return lax.ppermute(x, ("tm", "space"), pairs)


def rolled(x, by):
    return pltpu.roll(x, by % x.shape[-1], x.ndim - 1)


def pack(place, inten, *outs):
    acqs, cols, rows = inten.shape
    tiles, blocks = len(outs), outs[0].shape[0]
    tile = rows // tiles
    wide = tile // LANES
    sides = blocks - cols * wide
    lane = lax.broadcasted_iota(jnp.int32, (1, LANES), 1)
    slot = lane // MARGIN
    for d, out in enumerate(outs):
        t = place[0] + d
        t = jnp.where(t >= tiles, t - tiles, t)
        start = t * tile
        after = jnp.minimum(start + tile, rows - LANES)
        before = jnp.maximum(start - LANES, 0)
        right = jnp.zeros((acqs, LANES), jnp.float32)
        left = right
        for c in range(cols):
            main = jnp.log(inten[:, c, pl.ds(pl.multiple_of(start, LANES), tile)])
            for k in range(wide):
                out[c * wide + k] = main[:, k * LANES : (k + 1) * LANES].astype(jnp.bfloat16)
            if sides == 1:
                near = pl.multiple_of(jnp.where(t == 0, after, before), LANES)
                edge = jnp.log(inten[:, c, pl.ds(near, LANES)])
                edge = jnp.where(t == 0, rolled(edge, c * MARGIN), rolled(edge, (c + 1) * MARGIN))
                right = jnp.where(slot == c, edge, right)
            else:
                edge = jnp.log(inten[:, c, pl.ds(pl.multiple_of(after, LANES), LANES)])
                right = jnp.where(slot == c, rolled(edge, c * MARGIN), right)
                edge = jnp.log(inten[:, c, pl.ds(pl.multiple_of(before, LANES), LANES)])
                left = jnp.where(slot == c, rolled(edge, (c + 1) * MARGIN), left)
        out[cols * wide] = right.astype(jnp.bfloat16)
        if sides == 2:
            out[cols * wide + 1] = left.astype(jnp.bfloat16)


def body(place, own, mate, next_to, extra, across, w1, wr, out, inten, act_a, act_b):
    acqs = own.shape[1]
    channels, cols, tile = out.shape
    wide = tile // LANES
    sides = own.shape[0] - cols * wide
    width = tile + LANES
    first_col, all_cols = place[0], place[1]
    base, all_rows = place[2], place[3]
    odd = place[4] == 1

    lane = lax.broadcasted_iota(jnp.int32, (1, width), 1)
    row = jnp.where(lane < tile + LANES // 2, lane, lane - width)
    inside = (row >= -MARGIN) & (row < tile + MARGIN)
    row = row + base
    inside = inside & (row >= 0) & (row < all_rows)
    row_mask = inside.astype(jnp.float32)
    early = lax.broadcasted_iota(jnp.int32, (1, LANES), 1) < LANES // 2
    lowest = base == 0

    def column(ref, k, c, count):
        parts = [ref[k * wide + n].astype(jnp.float32) for n in range(wide)]
        right = ref[count * wide].astype(jnp.float32)
        if sides == 1:
            to_left = rolled(right, -(c + 1) * MARGIN)
            right = jnp.where(lowest, rolled(right, -c * MARGIN), to_left)
        else:
            left = rolled(ref[count * wide + 1].astype(jnp.float32), -(c + 1) * MARGIN)
            right = jnp.where(early, rolled(right, -c * MARGIN), left)
        return jnp.concatenate(parts + [right], axis=1)

    more = HALO - cols
    pieces = [(extra, across, odd, more, cols - more), (next_to, mate, odd, cols, 0), (own, own, None, cols, 0)]
    pieces += [(mate, next_to, odd, cols, 0), (across, extra, odd, more, 0)]
    at = 0
    for ref, other, use_other, count, first in pieces:
        for k in range(count):
            ok = inside
            if use_other is None:
                coded = column(ref, k, first + k, count)
            else:
                coded = jnp.where(use_other, column(other, k, first + k, count), column(ref, k, first + k, count))
                g = first_col - HALO + at
                ok = ok & (g >= 0) & (g < all_cols)
            inten[at] = jnp.where(ok, jnp.exp(coded), 0.0)
            at += 1

    row_count = jnp.minimum(row + RADIUS, all_rows - 1) - jnp.maximum(row - RADIUS, 0) + 1
    row_count = jnp.maximum(row_count, 1).astype(jnp.float32)
    feature_cols = cols + 2 * LAYERS

    def despeckle(f, _):
        total = inten[f]
        for k in range(1, 2 * RADIUS + 1):
            total = total + inten[f + k]
        three = rolled(total, 1) + total + rolled(total, -1)
        box = rolled(three, 2) + total + rolled(three, -2)
        g = first_col - LAYERS + f
        col_count = jnp.minimum(g + RADIUS, all_cols - 1) - jnp.maximum(g - RADIUS, 0) + 1
        col_count = jnp.maximum(col_count, 1).astype(jnp.float32)
        local_mean = box * (1.0 / (row_count * col_count))
        ratio = jnp.sum(inten[f + RADIUS] / local_mean, axis=0, keepdims=True)
        feature = jnp.log(local_mean) + jnp.log(ratio / acqs)
        ok = (g >= 0) & (g < all_cols)
        feature = jnp.where(inside & ok, feature, 0.0).astype(jnp.bfloat16)
        to = pl.multiple_of(f * 3 * acqs, 16)
        act_a[pl.ds(to, acqs), :] = rolled(feature, 1)
        act_a[pl.ds(to + acqs, acqs), :] = feature
        act_a[pl.ds(to + 2 * acqs, acqs), :] = rolled(feature, -1)
        return 0

    lax.fori_loop(0, feature_cols, despeckle, 0, unroll=4)

    source, target = act_a, act_b
    depth = acqs
    for layer in range(LAYERS):
        weight = w1[...] if layer == 0 else wr[layer - 1]
        out_cols = feature_cols - 2 * (layer + 1)
        last = layer == LAYERS - 1
        span = tile if last else width
        for start in range(0, out_cols, PAIR * BESIDE):
            firsts = range(start, min(start + PAIR * BESIDE, out_cols), PAIR)
            taps = [source[j * 3 * depth : (j + PAIR + 2) * 3 * depth, :span] for j in firsts]
            summed = jnp.dot(weight, jnp.concatenate(taps, axis=1), preferred_element_type=jnp.float32)
            for n, j in enumerate(firsts):
                for p in range(PAIR):
                    column_sum = summed[p * channels : (p + 1) * channels, n * span : (n + 1) * span]
                    if last:
                        out[:, j + p, :] = column_sum
                        continue
                    g = first_col - (LAYERS - 1 - layer) + j + p
                    ok = ((g >= 0) & (g < all_cols)).astype(jnp.float32)
                    hidden = (jnp.maximum(column_sum, 0.0) * (row_mask * ok)).astype(jnp.bfloat16)
                    to = (j + p) * 3 * channels
                    target[to : to + channels, :] = rolled(hidden, 1)
                    target[to + channels : to + 2 * channels, :] = hidden
                    target[to + 2 * channels : to + 3 * channels, :] = rolled(hidden, -1)
        source, target = target, source
        depth = channels


def shards(intensity, w_first, w_rest):
    acqs_own, cols, rows = intensity.shape
    tm = lax.axis_size("tm")
    space = lax.axis_size("space")
    m = lax.axis_index("tm")
    s = lax.axis_index("space")
    tile = rows // tm
    wide = tile // LANES
    channels, acqs = w_first.shape[2:]
    vmem = pl.BlockSpec(memory_space=pltpu.VMEM)
    smem = pl.BlockSpec(memory_space=pltpu.SMEM)

    blocks = cols * wide + (1 if tm == 2 else 2)
    packed = pl.pallas_call(
        pack,
        out_shape=[jax.ShapeDtypeStruct((blocks, acqs_own, LANES), jnp.bfloat16)] * tm,
        in_specs=[smem, vmem],
        out_specs=[vmem] * tm,
        compiler_params=pltpu.CompilerParams(vmem_limit_bytes=8 * 1024 * 1024),
    )(jnp.reshape(m, (1,)).astype(jnp.int32), intensity)
    parts = [packed[0]]
    for d in range(1, tm):
        parts.append(lax.ppermute(packed[d], "tm", [(i, (i + d) % tm) for i in range(tm)]))
    evens = list(range(0, space, 2))
    odds = [i - 1 for i in evens[1:]]
    beside = [swapped(packed[0], odds, 1)]
    own = jnp.concatenate(parts, axis=1)
    mate = swapped(own, evens, 1)

    far = HALO - cols
    odd = s % 2 == 1
    edges = mate[cols * wide :]
    head = jnp.concatenate([mate[: far * wide], edges], axis=0)
    tail = jnp.concatenate([mate[(cols - far) * wide : cols * wide], edges], axis=0)
    near, across = jnp.where(odd, tail, head), jnp.where(odd, head, tail)
    onward = parts[1:] + [near[:, d * acqs_own : (d + 1) * acqs_own] for d in range(tm)]
    counts = [x.shape[0] for x in onward]
    onward, across = lax.optimization_barrier((jnp.concatenate(onward, axis=0), across))
    onward = swapped(onward, odds, 1)
    across = swapped(across, evens[:-1], 3)
    arrived, start = [], 0
    for count in counts:
        arrived.append(onward[start : start + count])
        start += count
    beside = jnp.concatenate(beside + arrived[: tm - 1], axis=1)
    extra = jnp.concatenate(arrived[tm - 1 :], axis=1)

    def spread(w):
        step = w.shape[-1] // 3
        rest = [(0, 0)] * (w.ndim - 1)
        moved = [jnp.pad(w, rest + [(p * step, (PAIR - 1 - p) * step)]) for p in range(PAIR)]
        return jnp.concatenate(moved, axis=-2)

    order = (m - jnp.arange(tm)) % tm
    w1 = jnp.take(w_first.reshape(3, 3, channels, tm, acqs_own), order, axis=3)
    w1 = spread(w1.reshape(3, 3, channels, acqs).transpose(2, 0, 1, 3).reshape(channels, 9 * acqs))
    wr = spread(w_rest.transpose(0, 3, 1, 2, 4).reshape(LAYERS - 1, channels, 9 * channels))

    place = jnp.stack(
        [s * cols, jnp.int32(cols * space), m * tile, jnp.int32(rows), s % 2]
    ).astype(jnp.int32)
    width = tile + LANES
    act = ((cols + 2 * LAYERS) * 3 * channels, width)
    return pl.pallas_call(
        body,
        out_shape=jax.ShapeDtypeStruct((channels, cols, tile), jnp.float32),
        in_specs=[smem] + [vmem] * 7,
        out_specs=vmem,
        scratch_shapes=[
            pltpu.VMEM((cols + 2 * HALO, acqs, width), jnp.float32),
            pltpu.VMEM(act, jnp.bfloat16),
            pltpu.VMEM(act, jnp.bfloat16),
        ],
        compiler_params=pltpu.CompilerParams(vmem_limit_bytes=20 * 1024 * 1024),
    )(place, own, mate, beside, extra, across, w1, wr)


def solution(mesh):
    in_specs = (P("tm", "space", None), P(), P())
    out_specs = P(None, "space", "tm")
    return jax.shard_map(shards, mesh=mesh, in_specs=in_specs, out_specs=out_specs, check_vma=False)
```

```python
import jax
import jax.numpy as jnp
from jax import lax
from jax.experimental import pallas as pl
from jax.experimental.pallas import tpu as pltpu
from jax.sharding import PartitionSpec as P

LAYERS = 6
RADIUS = 3
HALO = RADIUS + LAYERS
MARGIN = 16
LANES = 128
PAIR = 2
BESIDE = 2


def swapped(x, lows, by):
    size, groups = lax.axis_size("space"), lax.axis_size("tm")
    partner = {i: i + by for i in lows} | {i + by: i for i in lows}
    alone = [i for i in range(size) if i not in partner]
    pairs = [(g * size + i, g * size + j) for g in range(groups) for i, j in partner.items()]
    if groups % 2 == 0:
        pairs += [(g * size + i, (g ^ 1) * size + i) for g in range(groups) for i in alone]
    else:
        pairs += [
            (g * size + i, g * size + j) for g in range(groups) for i, j in zip(alone, reversed(alone))
        ]
    return lax.ppermute(x, ("tm", "space"), pairs)


def rolled(x, by):
    return pltpu.roll(x, by % x.shape[-1], x.ndim - 1)


def pack(place, inten, *outs):
    acqs, cols, rows = inten.shape
    tiles, blocks = len(outs), outs[0].shape[0]
    tile = rows // tiles
    wide = tile // LANES
    sides = blocks - cols * wide
    lane = lax.broadcasted_iota(jnp.int32, (1, LANES), 1)
    slot = lane // MARGIN
    for d, out in enumerate(outs):
        t = place[0] + d
        t = jnp.where(t >= tiles, t - tiles, t)
        start = t * tile
        after = jnp.minimum(start + tile, rows - LANES)
        before = jnp.maximum(start - LANES, 0)
        right = jnp.zeros((acqs, LANES), jnp.float32)
        left = right
        for c in range(cols):
            main = jnp.log(inten[:, c, pl.ds(pl.multiple_of(start, LANES), tile)])
            for k in range(wide):
                out[c * wide + k] = main[:, k * LANES : (k + 1) * LANES].astype(jnp.bfloat16)
            if sides == 1:
                near = pl.multiple_of(jnp.where(t == 0, after, before), LANES)
                edge = jnp.log(inten[:, c, pl.ds(near, LANES)])
                edge = jnp.where(t == 0, rolled(edge, c * MARGIN), rolled(edge, (c + 1) * MARGIN))
                right = jnp.where(slot == c, edge, right)
            else:
                edge = jnp.log(inten[:, c, pl.ds(pl.multiple_of(after, LANES), LANES)])
                right = jnp.where(slot == c, rolled(edge, c * MARGIN), right)
                edge = jnp.log(inten[:, c, pl.ds(pl.multiple_of(before, LANES), LANES)])
                left = jnp.where(slot == c, rolled(edge, (c + 1) * MARGIN), left)
        out[cols * wide] = right.astype(jnp.bfloat16)
        if sides == 2:
            out[cols * wide + 1] = left.astype(jnp.bfloat16)


class Window:
    def __init__(self, place, cols, tile, acqs):
        self.cols, self.tile, self.acqs = cols, tile, acqs
        self.width = width = tile + LANES
        self.first, self.all_cols = place[0], place[1]
        self.base, self.all_rows = place[2], place[3]
        self.odd = place[4] == 1
        lane = lax.broadcasted_iota(jnp.int32, (1, width), 1)
        row = jnp.where(lane < tile + LANES // 2, lane, lane - width)
        inside = (row >= -MARGIN) & (row < tile + MARGIN)
        self.row = row + self.base
        self.inside = inside & (self.row >= 0) & (self.row < self.all_rows)
        self.row_mask = self.inside.astype(jnp.float32)
        count = jnp.minimum(self.row + RADIUS, self.all_rows - 1) - jnp.maximum(self.row - RADIUS, 0) + 1
        self.row_count = jnp.maximum(count, 1).astype(jnp.float32)

    def place_of(self, u):
        return self.first + jnp.where(self.odd, self.cols + HALO - 1 - u, u - HALO)

    def within(self, u):
        g = self.place_of(u)
        return (g >= 0) & (g < self.all_cols)

    def intensity(self, ref, k, slot, count, known):
        wide = self.tile // LANES
        k = jnp.where(self.odd, count - 1 - k, k)
        slot = jnp.where(self.odd, self.cols - 1 - slot, slot)
        parts = [ref[k * wide + n].astype(jnp.float32) for n in range(wide)]
        to_right = (self.cols - slot) * MARGIN % LANES
        to_left = (self.cols - slot - 1) * MARGIN % LANES
        edge = ref[count * wide].astype(jnp.float32)
        if ref.shape[0] == count * wide + 1:
            edge = pltpu.roll(edge, jnp.where(self.base == 0, to_right, to_left), 1)
        else:
            early = lax.broadcasted_iota(jnp.int32, (1, LANES), 1) < LANES // 2
            before = pltpu.roll(ref[count * wide + 1].astype(jnp.float32), to_left, 1)
            edge = jnp.where(early, pltpu.roll(edge, to_right, 1), before)
        coded = jnp.concatenate(parts + [edge], axis=1)
        ok = self.inside if known is None else self.inside & self.within(known)
        return jnp.where(ok, jnp.exp(coded), 0.0)

    def feature(self, u, inten):
        total = inten(u - RADIUS)
        for k in range(1 - RADIUS, RADIUS + 1):
            total = total + inten(u + k)
        three = rolled(total, 1) + total + rolled(total, -1)
        box = rolled(three, 2) + total + rolled(three, -2)
        g = self.place_of(u)
        count = jnp.minimum(g + RADIUS, self.all_cols - 1) - jnp.maximum(g - RADIUS, 0) + 1
        count = jnp.maximum(count, 1).astype(jnp.float32)
        local_mean = box * (1.0 / (self.row_count * count))
        ratio = jnp.sum(inten(u) / local_mean, axis=0, keepdims=True)
        feature = jnp.log(local_mean) + jnp.log(ratio / self.acqs)
        return jnp.where(self.inside & self.within(u), feature, 0.0).astype(jnp.bfloat16)

    def hidden(self, u, summed):
        ok = self.within(u).astype(jnp.float32)
        return (jnp.maximum(summed, 0.0) * (self.row_mask * ok)).astype(jnp.bfloat16)


def put(ref, k, value):
    depth = value.shape[0]
    to = k * 3 * depth
    ref[to : to + depth, :] = rolled(value, 1)
    ref[to + depth : to + 2 * depth, :] = value
    ref[to + 2 * depth : to + 3 * depth, :] = rolled(value, -1)


def columns(weight, wanted, source, channels, span, done):
    groups, at = [], 0
    while at < len(wanted):
        size = PAIR if wanted[at : at + PAIR] == list(range(wanted[at], wanted[at] + PAIR)) else 1
        groups.append((size, wanted[at]))
        at += size
    for size in (PAIR, 1):
        firsts = [j for n, j in groups if n == size]
        for start in range(0, len(firsts), BESIDE):
            some = firsts[start : start + BESIDE]
            taps = [jnp.concatenate([source(j + k, span) for k in range(size + 2)], axis=0) for j in some]
            used = weight if size == PAIR else weight[:channels, : taps[0].shape[0]]
            summed = jnp.dot(used, jnp.concatenate(taps, axis=1), preferred_element_type=jnp.float32)
            for n, j in enumerate(some):
                for p in range(size):
                    done(j + p, summed[p * channels : (p + 1) * channels, n * span : (n + 1) * span])


def chip_part(place, own, mate, w1, wr, inten, *layers):
    acqs, width = inten.shape[1:]
    cols = inten.shape[0] // 2
    tile = width - LANES
    channels = wr.shape[1] // PAIR
    win = Window(place, cols, tile, acqs)
    for k in range(cols):
        inten[k] = win.intensity(own, k, k, cols, None)
        inten[cols + k] = win.intensity(mate, k, k, cols, None)
    known = 2 * cols
    features = known - 2 * RADIUS
    for k in range(features):
        put(layers[0], k, win.feature(HALO + RADIUS + k, lambda u: inten[u - HALO]))
    for layer in range(len(layers) - 1):
        left = features - 2 * (layer + 1)
        depth = acqs if layer == 0 else channels

        def source(j, span, ref=layers[layer], depth=depth):
            return ref[j * 3 * depth : (j + 1) * 3 * depth, :span]

        def done(j, summed, layer=layer):
            put(layers[layer + 1], j, win.hidden(HALO + RADIUS + layer + 1 + j, summed))

        weight = w1[...] if layer == 0 else wr[layer - 1]
        columns(weight, list(range(left)), source, channels, width, done)


def rest_part(place, next_to, extra, across, w1, wr, chip, *refs):
    acqs, width = chip.shape[1:]
    count = chip_layers(chip.shape[0] // 2)
    given, out, inten, results, mine = refs[:count], refs[count], refs[count + 1], refs[count + 2], refs[count + 3 :]
    channels, cols, tile = out.shape
    win = Window(place, cols, tile, acqs)
    more = HALO - cols
    for k in range(more):
        inten[k] = win.intensity(extra, k, cols - more + k, more, k)
        inten[HALO + k] = win.intensity(across, k, k, more, HALO + 2 * cols + k)
    for k in range(cols):
        inten[more + k] = win.intensity(next_to, k, k, cols, more + k)

    def intensity(u):
        if HALO <= u < HALO + 2 * cols:
            return chip[u - HALO]
        return inten[u if u < HALO else u - 2 * cols]

    first = HALO
    for layer in range(LAYERS + 1):
        total = cols + 2 * (LAYERS - layer)
        have = max(2 * cols - 2 * RADIUS - 2 * layer, 0) if layer < count else 0
        wanted = [j for j in range(total) if not first <= j < first + have]
        if layer == 0:
            for k, f in enumerate(wanted):
                put(mine[0], k, win.feature(RADIUS + f, intensity))
        else:
            weight = w1[...] if layer == 1 else wr[layer - 2]

            def done(j, summed, layer=layer, wanted=wanted):
                if layer < LAYERS:
                    put(mine[layer], wanted.index(j), win.hidden(RADIUS + layer + j, summed))
                else:
                    results[jnp.where(win.odd, cols - 1 - j, j)] = summed

            columns(weight, wanted, source, channels, tile if layer == LAYERS else width, done)
        depth = acqs if layer == 0 else channels

        def source(j, span, layer=layer, depth=depth, wanted=wanted):
            if j in wanted:
                ref, k = mine[layer], wanted.index(j)
            else:
                ref, k = given[layer], j - first
            return ref[k * 3 * depth : (k + 1) * 3 * depth, :span]

    for j in range(cols):
        out[:, j, :] = results[j]


def chip_layers(cols):
    return min(LAYERS, cols - RADIUS)


def shards(intensity, w_first, w_rest):
    acqs_own, cols, rows = intensity.shape
    tm = lax.axis_size("tm")
    space = lax.axis_size("space")
    m = lax.axis_index("tm")
    s = lax.axis_index("space")
    tile = rows // tm
    wide = tile // LANES
    channels, acqs = w_first.shape[2:]
    vmem = pl.BlockSpec(memory_space=pltpu.VMEM)
    smem = pl.BlockSpec(memory_space=pltpu.SMEM)

    blocks = cols * wide + (1 if tm == 2 else 2)
    packed = pl.pallas_call(
        pack,
        out_shape=[jax.ShapeDtypeStruct((blocks, acqs_own, LANES), jnp.bfloat16)] * tm,
        in_specs=[smem, vmem],
        out_specs=[vmem] * tm,
        compiler_params=pltpu.CompilerParams(vmem_limit_bytes=8 * 1024 * 1024),
    )(jnp.reshape(m, (1,)).astype(jnp.int32), intensity)
    parts = [packed[0]]
    for d in range(1, tm):
        parts.append(lax.ppermute(packed[d], "tm", [(i, (i + d) % tm) for i in range(tm)]))
    evens = list(range(0, space, 2))
    odds = [i - 1 for i in evens[1:]]
    beside = [swapped(packed[0], odds, 1)]
    own = jnp.concatenate(parts, axis=1)
    mate = swapped(own, evens, 1)

    far = HALO - cols
    odd = s % 2 == 1

    def ends(x):
        edges = x[cols * wide :]
        head = jnp.concatenate([x[: far * wide], edges], axis=0)
        tail = jnp.concatenate([x[(cols - far) * wide : cols * wide], edges], axis=0)
        return head, tail

    head, tail = ends(own)
    ring = [(i, i - 2 if i else 1) for i in evens] + [(i + 1, i + 3 if i + 3 < space else i) for i in evens]
    across = lax.ppermute(jnp.where(odd, tail, head), "space", ring)
    head, tail = ends(mate)
    near = jnp.where(odd, tail, head)
    onward = parts[1:] + [near[:, d * acqs_own : (d + 1) * acqs_own] for d in range(tm)]
    counts = [x.shape[0] for x in onward]
    onward = swapped(jnp.concatenate(onward, axis=0), odds, 1)
    arrived, start = [], 0
    for count in counts:
        arrived.append(onward[start : start + count])
        start += count
    beside = jnp.concatenate(beside + arrived[: tm - 1], axis=1)
    extra = jnp.concatenate(arrived[tm - 1 :], axis=1)

    def spread(w):
        step = w.shape[-1] // 3
        rest = [(0, 0)] * (w.ndim - 1)
        moved = [jnp.pad(w, rest + [(p * step, (PAIR - 1 - p) * step)]) for p in range(PAIR)]
        return jnp.concatenate(moved, axis=-2)

    w_first = jnp.where(odd, w_first[::-1], w_first)
    w_rest = jnp.where(odd, w_rest[:, ::-1], w_rest)
    order = (m - jnp.arange(tm)) % tm
    w1 = jnp.take(w_first.reshape(3, 3, channels, tm, acqs_own), order, axis=3)
    w1 = spread(w1.reshape(3, 3, channels, acqs).transpose(2, 0, 1, 3).reshape(channels, 9 * acqs))
    wr = spread(w_rest.transpose(0, 3, 1, 2, 4).reshape(LAYERS - 1, channels, 9 * channels))

    place = jnp.stack(
        [s * cols, jnp.int32(cols * space), m * tile, jnp.int32(rows), s % 2]
    ).astype(jnp.int32)
    width = tile + LANES
    limit = pltpu.CompilerParams(vmem_limit_bytes=20 * 1024 * 1024)
    inputs = chip_layers(cols)
    depths = [acqs] + [channels] * (LAYERS - 1)
    reach = [2 * cols - 2 * RADIUS - 2 * n for n in range(inputs)]
    chip, *given = pl.pallas_call(
        chip_part,
        out_shape=[jax.ShapeDtypeStruct((2 * cols, acqs, width), jnp.float32)]
        + [jax.ShapeDtypeStruct((reach[n] * 3 * depths[n], width), jnp.bfloat16) for n in range(inputs)],
        in_specs=[smem] + [vmem] * 4,
        out_specs=[vmem] * (1 + inputs),
        compiler_params=limit,
        cost_estimate=pl.CostEstimate(flops=10**9, bytes_accessed=4 * 10**6, transcendentals=10**6),
    )(place, own, mate, w1, wr)
    lacking = [cols + 2 * (LAYERS - n) - (reach[n] if n < inputs else 0) for n in range(LAYERS)]
    return pl.pallas_call(
        rest_part,
        out_shape=jax.ShapeDtypeStruct((channels, cols, tile), jnp.float32),
        in_specs=[smem] + [vmem] * (6 + inputs),
        out_specs=vmem,
        scratch_shapes=[
            pltpu.VMEM((2 * HALO - cols, acqs, width), jnp.float32),
            pltpu.VMEM((cols, channels, tile), jnp.float32),
        ]
        + [pltpu.VMEM((lacking[n] * 3 * depths[n], width), jnp.bfloat16) for n in range(LAYERS)],
        compiler_params=limit,
        cost_estimate=pl.CostEstimate(flops=2 * 10**9, bytes_accessed=4 * 10**6, transcendentals=10**6),
    )(place, beside, extra, across, w1, wr, chip, *given)


def solution(mesh):
    in_specs = (P("tm", "space", None), P(), P())
    out_specs = P(None, "space", "tm")
    return jax.shard_map(shards, mesh=mesh, in_specs=in_specs, out_specs=out_specs, check_vma=False)
```

```python
import functools

import jax
import jax.numpy as jnp
from jax import lax
from jax.experimental import pallas as pl
from jax.experimental.pallas import tpu as pltpu
from jax.sharding import PartitionSpec as P

LAYERS = 6
RADIUS = 3
HALO = RADIUS + LAYERS
MARGIN = 16
LANES = 128
PAIR = 2
BESIDE = 2


def swapped(x, lows, by):
    size, groups = lax.axis_size("space"), lax.axis_size("tm")
    partner = {i: i + by for i in lows} | {i + by: i for i in lows}
    alone = [i for i in range(size) if i not in partner]
    pairs = [(g * size + i, g * size + j) for g in range(groups) for i, j in partner.items()]
    if groups % 2 == 0:
        pairs += [(g * size + i, (g ^ 1) * size + i) for g in range(groups) for i in alone]
    else:
        pairs += [
            (g * size + i, g * size + j) for g in range(groups) for i, j in zip(alone, reversed(alone))
        ]
    return lax.ppermute(x, ("tm", "space"), pairs)


def rolled(x, by):
    return pltpu.roll(x, by % x.shape[-1], x.ndim - 1)


def pack(place, inten, *outs):
    acqs, cols, rows = inten.shape
    tiles, blocks = len(outs), outs[0].shape[0]
    tile = rows // tiles
    wide = tile // LANES
    sides = blocks - cols * wide
    lane = lax.broadcasted_iota(jnp.int32, (1, LANES), 1)
    slot = lane // MARGIN
    for d, out in enumerate(outs):
        t = place[0] + d
        t = jnp.where(t >= tiles, t - tiles, t)
        start = t * tile
        after = jnp.minimum(start + tile, rows - LANES)
        before = jnp.maximum(start - LANES, 0)
        right = jnp.zeros((acqs, LANES), jnp.float32)
        left = right
        for c in range(cols):
            main = jnp.log(inten[:, c, pl.ds(pl.multiple_of(start, LANES), tile)])
            for k in range(wide):
                out[c * wide + k] = main[:, k * LANES : (k + 1) * LANES].astype(jnp.bfloat16)
            if sides == 1:
                near = pl.multiple_of(jnp.where(t == 0, after, before), LANES)
                edge = jnp.log(inten[:, c, pl.ds(near, LANES)])
                edge = jnp.where(t == 0, rolled(edge, c * MARGIN), rolled(edge, (c + 1) * MARGIN))
                right = jnp.where(slot == c, edge, right)
            else:
                edge = jnp.log(inten[:, c, pl.ds(pl.multiple_of(after, LANES), LANES)])
                right = jnp.where(slot == c, rolled(edge, c * MARGIN), right)
                edge = jnp.log(inten[:, c, pl.ds(pl.multiple_of(before, LANES), LANES)])
                left = jnp.where(slot == c, rolled(edge, (c + 1) * MARGIN), left)
        out[cols * wide] = right.astype(jnp.bfloat16)
        if sides == 2:
            out[cols * wide + 1] = left.astype(jnp.bfloat16)


def spread(swap, place, w_first, w_rest, first, rest):
    channels, depth = w_first.shape[2:]

    def laid(pieces):
        step = 3 * pieces[0].shape[1]
        rows = []
        for p in range(PAIR):
            before = [jnp.zeros((channels, p * step), jnp.float32)] if p else []
            after = [jnp.zeros((channels, (PAIR - 1 - p) * step), jnp.float32)] if p < PAIR - 1 else []
            rows.append(jnp.concatenate(before + pieces + after, axis=1))
        return jnp.concatenate(rows, axis=0).astype(jnp.bfloat16)

    odd = place[4] == 1
    taps = [(a, b) for a in range(3) for b in range(3)]
    late = [(jnp.where(odd, 2 - a, a), b) for a, b in taps]
    pieces = [w_first[a, b].astype(jnp.float32) for a, b in taps]
    if swap:
        half = depth // 2
        moved = [jnp.concatenate([x[:, half:], x[:, :half]], axis=1) for x in pieces]
        pieces = [jnp.where(place[2] == 0, x, y) for x, y in zip(pieces, moved)]
    first[...] = laid(pieces)
    for layer in range(LAYERS - 1):
        rest[layer] = laid([w_rest[layer, a, b].astype(jnp.float32) for a, b in late])


class Window:
    def __init__(self, place, cols, tile, acqs):
        self.cols, self.tile, self.acqs = cols, tile, acqs
        self.width = width = tile + LANES
        self.first, self.all_cols = place[0], place[1]
        self.base, self.all_rows = place[2], place[3]
        self.odd = place[4] == 1
        lane = lax.broadcasted_iota(jnp.int32, (1, width), 1)
        row = jnp.where(lane < tile + LANES // 2, lane, lane - width)
        inside = (row >= -MARGIN) & (row < tile + MARGIN)
        self.row = row + self.base
        self.inside = inside & (self.row >= 0) & (self.row < self.all_rows)
        self.row_mask = self.inside.astype(jnp.float32)
        count = jnp.minimum(self.row + RADIUS, self.all_rows - 1) - jnp.maximum(self.row - RADIUS, 0) + 1
        self.row_count = jnp.maximum(count, 1).astype(jnp.float32)

    def place_of(self, u):
        return self.first + jnp.where(self.odd, self.cols + HALO - 1 - u, u - HALO)

    def within(self, u):
        g = self.place_of(u)
        return (g >= 0) & (g < self.all_cols)

    def intensity(self, ref, k, slot, count, known):
        wide = self.tile // LANES
        k = jnp.where(self.odd, count - 1 - k, k)
        slot = jnp.where(self.odd, self.cols - 1 - slot, slot)
        parts = [ref[k * wide + n].astype(jnp.float32) for n in range(wide)]
        to_right = (self.cols - slot) * MARGIN % LANES
        to_left = (self.cols - slot - 1) * MARGIN % LANES
        edge = ref[count * wide].astype(jnp.float32)
        if ref.shape[0] == count * wide + 1:
            edge = pltpu.roll(edge, jnp.where(self.base == 0, to_right, to_left), 1)
        else:
            early = lax.broadcasted_iota(jnp.int32, (1, LANES), 1) < LANES // 2
            before = pltpu.roll(ref[count * wide + 1].astype(jnp.float32), to_left, 1)
            edge = jnp.where(early, pltpu.roll(edge, to_right, 1), before)
        coded = jnp.concatenate(parts + [edge], axis=1)
        ok = self.inside if known is None else self.inside & self.within(known)
        return jnp.where(ok, jnp.exp(coded), 0.0)

    def feature(self, u, inten):
        total = inten(u - RADIUS)
        for k in range(1 - RADIUS, RADIUS + 1):
            total = total + inten(u + k)
        three = rolled(total, 1) + total + rolled(total, -1)
        box = rolled(three, 2) + total + rolled(three, -2)
        g = self.place_of(u)
        count = jnp.minimum(g + RADIUS, self.all_cols - 1) - jnp.maximum(g - RADIUS, 0) + 1
        count = jnp.maximum(count, 1).astype(jnp.float32)
        local_mean = box * (1.0 / (self.row_count * count))
        ratio = jnp.sum(inten(u) / local_mean, axis=0, keepdims=True)
        feature = jnp.log(local_mean) + jnp.log(ratio / self.acqs)
        return jnp.where(self.inside & self.within(u), feature, 0.0).astype(jnp.bfloat16)

    def hidden(self, u, summed):
        ok = self.within(u).astype(jnp.float32)
        return (jnp.maximum(summed, 0.0) * (self.row_mask * ok)).astype(jnp.bfloat16)


def put(ref, k, value):
    depth = value.shape[0]
    to = k * 3 * depth
    ref[to : to + depth, :] = rolled(value, 1)
    ref[to + depth : to + 2 * depth, :] = value
    ref[to + 2 * depth : to + 3 * depth, :] = rolled(value, -1)


def columns(weight, wanted, source, channels, span, done):
    groups, at = [], 0
    while at < len(wanted):
        size = PAIR if wanted[at : at + PAIR] == list(range(wanted[at], wanted[at] + PAIR)) else 1
        groups.append((size, wanted[at]))
        at += size
    for size in (PAIR, 1):
        firsts = [j for n, j in groups if n == size]
        for start in range(0, len(firsts), BESIDE):
            some = firsts[start : start + BESIDE]
            taps = [jnp.concatenate([source(j + k, span) for k in range(size + 2)], axis=0) for j in some]
            used = weight if size == PAIR else weight[:channels, : taps[0].shape[0]]
            summed = jnp.dot(used, jnp.concatenate(taps, axis=1), preferred_element_type=jnp.float32)
            for n, j in enumerate(some):
                for p in range(size):
                    done(j + p, summed[p * channels : (p + 1) * channels, n * span : (n + 1) * span])


def chip_part(place, own, mate, w1, wr, inten, *layers):
    acqs, width = inten.shape[1:]
    cols = inten.shape[0] // 2
    tile = width - LANES
    channels = wr.shape[1] // PAIR
    win = Window(place, cols, tile, acqs)
    for k in range(cols):
        inten[k] = win.intensity(own, k, k, cols, None)
        inten[cols + k] = win.intensity(mate, k, k, cols, None)
    known = 2 * cols
    features = known - 2 * RADIUS
    for k in range(features):
        put(layers[0], k, win.feature(HALO + RADIUS + k, lambda u: inten[u - HALO]))
    for layer in range(len(layers) - 1):
        left = features - 2 * (layer + 1)
        depth = acqs if layer == 0 else channels

        def source(j, span, ref=layers[layer], depth=depth):
            return ref[j * 3 * depth : (j + 1) * 3 * depth, :span]

        def done(j, summed, layer=layer):
            put(layers[layer + 1], j, win.hidden(HALO + RADIUS + layer + 1 + j, summed))

        weight = w1[...] if layer == 0 else wr[layer - 1]
        columns(weight, list(range(left)), source, channels, width, done)


def rest_part(place, next_to, extra, across, w1, wr, chip, *refs):
    acqs, width = chip.shape[1:]
    count = chip_layers(chip.shape[0] // 2)
    given, out, inten, results, mine = refs[:count], refs[count], refs[count + 1], refs[count + 2], refs[count + 3 :]
    channels, cols, tile = out.shape
    win = Window(place, cols, tile, acqs)
    more = HALO - cols
    for k in range(more):
        inten[k] = win.intensity(extra, k, cols - more + k, more, k)
        inten[HALO + k] = win.intensity(across, k, k, more, HALO + 2 * cols + k)
    for k in range(cols):
        inten[more + k] = win.intensity(next_to, k, k, cols, more + k)

    def intensity(u):
        if HALO <= u < HALO + 2 * cols:
            return chip[u - HALO]
        return inten[u if u < HALO else u - 2 * cols]

    first = HALO
    for layer in range(LAYERS + 1):
        total = cols + 2 * (LAYERS - layer)
        have = max(2 * cols - 2 * RADIUS - 2 * layer, 0) if layer < count else 0
        wanted = [j for j in range(total) if not first <= j < first + have]
        if layer == 0:
            for k, f in enumerate(wanted):
                put(mine[0], k, win.feature(RADIUS + f, intensity))
        else:
            weight = w1[...] if layer == 1 else wr[layer - 2]

            def done(j, summed, layer=layer, wanted=wanted):
                if layer < LAYERS:
                    put(mine[layer], wanted.index(j), win.hidden(RADIUS + layer + j, summed))
                else:
                    results[jnp.where(win.odd, cols - 1 - j, j)] = summed

            columns(weight, wanted, source, channels, tile if layer == LAYERS else width, done)
        depth = acqs if layer == 0 else channels

        def source(j, span, layer=layer, depth=depth, wanted=wanted):
            if j in wanted:
                ref, k = mine[layer], wanted.index(j)
            else:
                ref, k = given[layer], j - first
            return ref[k * 3 * depth : (k + 1) * 3 * depth, :span]

    for j in range(cols):
        out[:, j, :] = results[j]


def chip_layers(cols):
    return min(LAYERS, cols - RADIUS)


def shards(intensity, w_first, w_rest):
    acqs_own, cols, rows = intensity.shape
    tm = lax.axis_size("tm")
    space = lax.axis_size("space")
    m = lax.axis_index("tm")
    s = lax.axis_index("space")
    tile = rows // tm
    wide = tile // LANES
    channels, acqs = w_first.shape[2:]
    vmem = pl.BlockSpec(memory_space=pltpu.VMEM)
    smem = pl.BlockSpec(memory_space=pltpu.SMEM)

    blocks = cols * wide + (1 if tm == 2 else 2)
    packed = pl.pallas_call(
        pack,
        out_shape=[jax.ShapeDtypeStruct((blocks, acqs_own, LANES), jnp.bfloat16)] * tm,
        in_specs=[smem, vmem],
        out_specs=[vmem] * tm,
        compiler_params=pltpu.CompilerParams(vmem_limit_bytes=8 * 1024 * 1024),
    )(jnp.reshape(m, (1,)).astype(jnp.int32), intensity)
    parts = [packed[0]]
    for d in range(1, tm):
        parts.append(lax.ppermute(packed[d], "tm", [(i, (i + d) % tm) for i in range(tm)]))
    evens = list(range(0, space, 2))
    odds = [i - 1 for i in evens[1:]]
    beside = [swapped(packed[0], odds, 1)]
    own = jnp.concatenate(parts, axis=1)
    odd = s % 2 == 1
    w_first = jnp.where(odd, w_first[::-1], w_first)
    own, w_first = lax.optimization_barrier((own, w_first))
    mate = swapped(own, evens, 1)

    far = HALO - cols
    odd = s % 2 == 1

    def ends(x):
        edges = x[cols * wide :]
        head = jnp.concatenate([x[: far * wide], edges], axis=0)
        tail = jnp.concatenate([x[(cols - far) * wide : cols * wide], edges], axis=0)
        return head, tail

    head, tail = ends(own)
    ring = [(i, i - 2 if i else 1) for i in evens] + [(i + 1, i + 3 if i + 3 < space else i) for i in evens]
    across = lax.ppermute(jnp.where(odd, tail, head), "space", ring)
    head, tail = ends(mate)
    near = jnp.where(odd, tail, head)
    onward = parts[1:] + [near[:, d * acqs_own : (d + 1) * acqs_own] for d in range(tm)]
    counts = [x.shape[0] for x in onward]
    onward = swapped(jnp.concatenate(onward, axis=0), odds, 1)
    arrived, start = [], 0
    for count in counts:
        arrived.append(onward[start : start + count])
        start += count
    beside = jnp.concatenate(beside + arrived[: tm - 1], axis=1)
    extra = jnp.concatenate(arrived[tm - 1 :], axis=1)

    place = jnp.stack(
        [s * cols, jnp.int32(cols * space), m * tile, jnp.int32(rows), s % 2]
    ).astype(jnp.int32)
    if tm != 2:
        order = (m - jnp.arange(tm)) % tm
        w_first = jnp.take(w_first.reshape(3, 3, channels, tm, acqs_own), order, axis=3)
        w_first = w_first.reshape(3, 3, channels, acqs)
    w1, wr = pl.pallas_call(
        functools.partial(spread, tm == 2),
        out_shape=[
            jax.ShapeDtypeStruct((PAIR * channels, 3 * (PAIR + 2) * acqs), jnp.bfloat16),
            jax.ShapeDtypeStruct((LAYERS - 1, PAIR * channels, 3 * (PAIR + 2) * channels), jnp.bfloat16),
        ],
        in_specs=[smem, vmem, vmem],
        out_specs=[vmem, vmem],
        compiler_params=pltpu.CompilerParams(vmem_limit_bytes=8 * 1024 * 1024),
        cost_estimate=pl.CostEstimate(flops=10**8, bytes_accessed=10**6, transcendentals=0),
    )(place, w_first, w_rest)
    width = tile + LANES
    limit = pltpu.CompilerParams(vmem_limit_bytes=20 * 1024 * 1024)
    inputs = chip_layers(cols)
    depths = [acqs] + [channels] * (LAYERS - 1)
    reach = [2 * cols - 2 * RADIUS - 2 * n for n in range(inputs)]
    chip, *given = pl.pallas_call(
        chip_part,
        out_shape=[jax.ShapeDtypeStruct((2 * cols, acqs, width), jnp.float32)]
        + [jax.ShapeDtypeStruct((reach[n] * 3 * depths[n], width), jnp.bfloat16) for n in range(inputs)],
        in_specs=[smem] + [vmem] * 4,
        out_specs=[vmem] * (1 + inputs),
        compiler_params=limit,
        cost_estimate=pl.CostEstimate(flops=10**9, bytes_accessed=4 * 10**6, transcendentals=10**6),
    )(place, own, mate, w1, wr)
    lacking = [cols + 2 * (LAYERS - n) - (reach[n] if n < inputs else 0) for n in range(LAYERS)]
    return pl.pallas_call(
        rest_part,
        out_shape=jax.ShapeDtypeStruct((channels, cols, tile), jnp.float32),
        in_specs=[smem] + [vmem] * (6 + inputs),
        out_specs=vmem,
        scratch_shapes=[
            pltpu.VMEM((2 * HALO - cols, acqs, width), jnp.float32),
            pltpu.VMEM((cols, channels, tile), jnp.float32),
        ]
        + [pltpu.VMEM((lacking[n] * 3 * depths[n], width), jnp.bfloat16) for n in range(LAYERS)],
        compiler_params=limit,
        cost_estimate=pl.CostEstimate(flops=2 * 10**9, bytes_accessed=4 * 10**6, transcendentals=10**6),
    )(place, beside, extra, across, w1, wr, chip, *given)


def solution(mesh):
    in_specs = (P("tm", "space", None), P(), P())
    out_specs = P(None, "space", "tm")
    return jax.shard_map(shards, mesh=mesh, in_specs=in_specs, out_specs=out_specs, check_vma=False)
```

```python
import functools

import jax
import jax.numpy as jnp
from jax import lax
from jax.experimental import pallas as pl
from jax.experimental.pallas import tpu as pltpu
from jax.sharding import PartitionSpec as P

LAYERS = 6
RADIUS = 3
HALO = RADIUS + LAYERS
MARGIN = 16
LANES = 128
PAIR = 2
BESIDE = 2


def swapped(x, lows, by):
    size, groups = lax.axis_size("space"), lax.axis_size("tm")
    partner = {i: i + by for i in lows} | {i + by: i for i in lows}
    alone = [i for i in range(size) if i not in partner]
    pairs = [(g * size + i, g * size + j) for g in range(groups) for i, j in partner.items()]
    if groups % 2 == 0:
        pairs += [(g * size + i, (g ^ 1) * size + i) for g in range(groups) for i in alone]
    else:
        pairs += [
            (g * size + i, g * size + j) for g in range(groups) for i, j in zip(alone, reversed(alone))
        ]
    return lax.ppermute(x, ("tm", "space"), pairs)


def rolled(x, by):
    return pltpu.roll(x, by % x.shape[-1], x.ndim - 1)


def pack(place, source, w_first, w_rest, first, rest, *refs):
    *outs, inten, sems = refs
    copies = [(source, inten), (w_first, first), (w_rest, rest)]
    copies = [pltpu.make_async_copy(x, y, sems.at[k]) for k, (x, y) in enumerate(copies)]
    for copy in copies:
        copy.start()
    acqs, cols, rows = inten.shape
    tiles, blocks = len(outs), outs[0].shape[0]
    copies[0].wait()
    tile = rows // tiles
    wide = tile // LANES
    sides = blocks - cols * wide
    lane = lax.broadcasted_iota(jnp.int32, (1, LANES), 1)
    slot = lane // MARGIN
    for d, out in enumerate(outs):
        t = place[0] + d
        t = jnp.where(t >= tiles, t - tiles, t)
        start = t * tile
        after = jnp.minimum(start + tile, rows - LANES)
        before = jnp.maximum(start - LANES, 0)
        right = jnp.zeros((acqs, LANES), jnp.float32)
        left = right
        for c in range(cols):
            main = jnp.log(inten[:, c, pl.ds(pl.multiple_of(start, LANES), tile)])
            for k in range(wide):
                out[c * wide + k] = main[:, k * LANES : (k + 1) * LANES].astype(jnp.bfloat16)
            if sides == 1:
                near = pl.multiple_of(jnp.where(t == 0, after, before), LANES)
                edge = jnp.log(inten[:, c, pl.ds(near, LANES)])
                edge = jnp.where(t == 0, rolled(edge, c * MARGIN), rolled(edge, (c + 1) * MARGIN))
                right = jnp.where(slot == c, edge, right)
            else:
                edge = jnp.log(inten[:, c, pl.ds(pl.multiple_of(after, LANES), LANES)])
                right = jnp.where(slot == c, rolled(edge, c * MARGIN), right)
                edge = jnp.log(inten[:, c, pl.ds(pl.multiple_of(before, LANES), LANES)])
                left = jnp.where(slot == c, rolled(edge, (c + 1) * MARGIN), left)
        out[cols * wide] = right.astype(jnp.bfloat16)
        if sides == 2:
            out[cols * wide + 1] = left.astype(jnp.bfloat16)
    for copy in copies[1:]:
        copy.wait()


def spread(swap, place, w_first, w_rest, first, rest):
    depth, channels = w_first.shape[2:]

    def laid(pieces):
        step = 3 * pieces[0].shape[1]
        rows = []
        for p in range(PAIR):
            before = [jnp.zeros((channels, p * step), jnp.float32)] if p else []
            after = [jnp.zeros((channels, (PAIR - 1 - p) * step), jnp.float32)] if p < PAIR - 1 else []
            rows.append(jnp.concatenate(before + pieces + after, axis=1))
        return jnp.concatenate(rows, axis=0).astype(jnp.bfloat16)

    odd = place[4] == 1
    taps = [(a, b) for a in range(3) for b in range(3)]
    late = [(jnp.where(odd, 2 - a, a), b) for a, b in taps]
    pieces = [w_first[a, b].astype(jnp.float32).T for a, b in late]
    if swap:
        half = depth // 2
        moved = [jnp.concatenate([x[:, half:], x[:, :half]], axis=1) for x in pieces]
        pieces = [jnp.where(place[2] == 0, x, y) for x, y in zip(pieces, moved)]
    first[...] = laid(pieces)
    for layer in range(LAYERS - 1):
        rest[layer] = laid([w_rest[layer, a, b].astype(jnp.float32) for a, b in late])


class Window:
    def __init__(self, place, cols, tile, acqs):
        self.cols, self.tile, self.acqs = cols, tile, acqs
        self.width = width = tile + LANES
        self.first, self.all_cols = place[0], place[1]
        self.base, self.all_rows = place[2], place[3]
        self.odd = place[4] == 1
        lane = lax.broadcasted_iota(jnp.int32, (1, width), 1)
        row = jnp.where(lane < tile + LANES // 2, lane, lane - width)
        inside = (row >= -MARGIN) & (row < tile + MARGIN)
        self.row = row + self.base
        self.inside = inside & (self.row >= 0) & (self.row < self.all_rows)
        self.row_mask = self.inside.astype(jnp.float32)
        count = jnp.minimum(self.row + RADIUS, self.all_rows - 1) - jnp.maximum(self.row - RADIUS, 0) + 1
        self.row_count = jnp.maximum(count, 1).astype(jnp.float32)

    def place_of(self, u):
        return self.first + jnp.where(self.odd, self.cols + HALO - 1 - u, u - HALO)

    def within(self, u):
        g = self.place_of(u)
        return (g >= 0) & (g < self.all_cols)

    def intensity(self, ref, k, slot, count, known):
        wide = self.tile // LANES
        k = jnp.where(self.odd, count - 1 - k, k)
        slot = jnp.where(self.odd, self.cols - 1 - slot, slot)
        parts = [ref[k * wide + n].astype(jnp.float32) for n in range(wide)]
        to_right = (self.cols - slot) * MARGIN % LANES
        to_left = (self.cols - slot - 1) * MARGIN % LANES
        edge = ref[count * wide].astype(jnp.float32)
        if ref.shape[0] == count * wide + 1:
            edge = pltpu.roll(edge, jnp.where(self.base == 0, to_right, to_left), 1)
        else:
            early = lax.broadcasted_iota(jnp.int32, (1, LANES), 1) < LANES // 2
            before = pltpu.roll(ref[count * wide + 1].astype(jnp.float32), to_left, 1)
            edge = jnp.where(early, pltpu.roll(edge, to_right, 1), before)
        coded = jnp.concatenate(parts + [edge], axis=1)
        ok = self.inside if known is None else self.inside & self.within(known)
        return jnp.where(ok, jnp.exp(coded), 0.0)

    def feature(self, u, inten):
        total = inten(u - RADIUS)
        for k in range(1 - RADIUS, RADIUS + 1):
            total = total + inten(u + k)
        three = rolled(total, 1) + total + rolled(total, -1)
        box = rolled(three, 2) + total + rolled(three, -2)
        g = self.place_of(u)
        count = jnp.minimum(g + RADIUS, self.all_cols - 1) - jnp.maximum(g - RADIUS, 0) + 1
        count = jnp.maximum(count, 1).astype(jnp.float32)
        local_mean = box * (1.0 / (self.row_count * count))
        ratio = jnp.sum(inten(u) / local_mean, axis=0, keepdims=True)
        feature = jnp.log(local_mean) + jnp.log(ratio / self.acqs)
        return jnp.where(self.inside & self.within(u), feature, 0.0).astype(jnp.bfloat16)

    def hidden(self, u, summed):
        ok = self.within(u).astype(jnp.float32)
        return (jnp.maximum(summed, 0.0) * (self.row_mask * ok)).astype(jnp.bfloat16)


def put(ref, k, value):
    depth = value.shape[0]
    to = k * 3 * depth
    ref[to : to + depth, :] = rolled(value, 1)
    ref[to + depth : to + 2 * depth, :] = value
    ref[to + 2 * depth : to + 3 * depth, :] = rolled(value, -1)


def columns(weight, wanted, source, channels, span, done):
    groups, at = [], 0
    while at < len(wanted):
        size = PAIR if wanted[at : at + PAIR] == list(range(wanted[at], wanted[at] + PAIR)) else 1
        groups.append((size, wanted[at]))
        at += size
    for size in (PAIR, 1):
        firsts = [j for n, j in groups if n == size]
        for start in range(0, len(firsts), BESIDE):
            some = firsts[start : start + BESIDE]
            taps = [jnp.concatenate([source(j + k, span) for k in range(size + 2)], axis=0) for j in some]
            used = weight if size == PAIR else weight[:channels, : taps[0].shape[0]]
            summed = jnp.dot(used, jnp.concatenate(taps, axis=1), preferred_element_type=jnp.float32)
            for n, j in enumerate(some):
                for p in range(size):
                    done(j + p, summed[p * channels : (p + 1) * channels, n * span : (n + 1) * span])


def chip_part(place, own, mate, w1, wr, inten, *layers):
    acqs, width = inten.shape[1:]
    cols = inten.shape[0] // 2
    tile = width - LANES
    channels = wr.shape[1] // PAIR
    win = Window(place, cols, tile, acqs)
    for k in range(cols):
        inten[k] = win.intensity(own, k, k, cols, None)
        inten[cols + k] = win.intensity(mate, k, k, cols, None)
    known = 2 * cols
    features = known - 2 * RADIUS
    for k in range(features):
        put(layers[0], k, win.feature(HALO + RADIUS + k, lambda u: inten[u - HALO]))
    for layer in range(len(layers) - 1):
        left = features - 2 * (layer + 1)
        depth = acqs if layer == 0 else channels

        def source(j, span, ref=layers[layer], depth=depth):
            return ref[j * 3 * depth : (j + 1) * 3 * depth, :span]

        def done(j, summed, layer=layer):
            put(layers[layer + 1], j, win.hidden(HALO + RADIUS + layer + 1 + j, summed))

        weight = w1[...] if layer == 0 else wr[layer - 1]
        columns(weight, list(range(left)), source, channels, width, done)


def rest_part(place, next_to, extra, across, w1, wr, chip, *refs):
    acqs, width = chip.shape[1:]
    count = chip_layers(chip.shape[0] // 2)
    given, out, inten, results, mine = refs[:count], refs[count], refs[count + 1], refs[count + 2], refs[count + 3 :]
    channels, cols, tile = out.shape
    win = Window(place, cols, tile, acqs)
    more = HALO - cols
    for k in range(more):
        inten[k] = win.intensity(extra, k, cols - more + k, more, k)
        inten[HALO + k] = win.intensity(across, k, k, more, HALO + 2 * cols + k)
    for k in range(cols):
        inten[more + k] = win.intensity(next_to, k, k, cols, more + k)

    def intensity(u):
        if HALO <= u < HALO + 2 * cols:
            return chip[u - HALO]
        return inten[u if u < HALO else u - 2 * cols]

    first = HALO
    for layer in range(LAYERS + 1):
        total = cols + 2 * (LAYERS - layer)
        have = max(2 * cols - 2 * RADIUS - 2 * layer, 0) if layer < count else 0
        wanted = [j for j in range(total) if not first <= j < first + have]
        if layer == 0:
            for k, f in enumerate(wanted):
                put(mine[0], k, win.feature(RADIUS + f, intensity))
        else:
            weight = w1[...] if layer == 1 else wr[layer - 2]

            def done(j, summed, layer=layer, wanted=wanted):
                if layer < LAYERS:
                    put(mine[layer], wanted.index(j), win.hidden(RADIUS + layer + j, summed))
                else:
                    results[jnp.where(win.odd, cols - 1 - j, j)] = summed

            columns(weight, wanted, source, channels, tile if layer == LAYERS else width, done)
        depth = acqs if layer == 0 else channels

        def source(j, span, layer=layer, depth=depth, wanted=wanted):
            if j in wanted:
                ref, k = mine[layer], wanted.index(j)
            else:
                ref, k = given[layer], j - first
            return ref[k * 3 * depth : (k + 1) * 3 * depth, :span]

    for j in range(cols):
        out[:, j, :] = results[j]


def chip_layers(cols):
    return min(LAYERS, cols - RADIUS)


def shards(intensity, w_first, w_rest):
    acqs_own, cols, rows = intensity.shape
    tm = lax.axis_size("tm")
    space = lax.axis_size("space")
    m = lax.axis_index("tm")
    s = lax.axis_index("space")
    tile = rows // tm
    wide = tile // LANES
    channels, acqs = w_first.shape[2:]
    vmem = pl.BlockSpec(memory_space=pltpu.VMEM)
    smem = pl.BlockSpec(memory_space=pltpu.SMEM)

    blocks = cols * wide + (1 if tm == 2 else 2)
    far_away = pl.BlockSpec(memory_space=pltpu.HBM)
    given = [intensity, w_first.transpose(0, 1, 3, 2), w_rest]
    w_first, w_rest, *packed = pl.pallas_call(
        pack,
        out_shape=[jax.ShapeDtypeStruct(x.shape, x.dtype) for x in given[1:]]
        + [jax.ShapeDtypeStruct((blocks, acqs_own, LANES), jnp.bfloat16)] * tm,
        in_specs=[smem] + [far_away] * 3,
        out_specs=[vmem] * (2 + tm),
        scratch_shapes=[pltpu.VMEM(intensity.shape, intensity.dtype), pltpu.SemaphoreType.DMA((3,))],
        compiler_params=pltpu.CompilerParams(vmem_limit_bytes=8 * 1024 * 1024),
    )(
        jnp.reshape(m, (1,)).astype(jnp.int32),
        *(pltpu.with_memory_space_constraint(x, pltpu.HBM) for x in given),
    )
    parts = [packed[0]]
    for d in range(1, tm):
        parts.append(lax.ppermute(packed[d], "tm", [(i, (i + d) % tm) for i in range(tm)]))
    evens = list(range(0, space, 2))
    odds = [i - 1 for i in evens[1:]]
    beside = [swapped(packed[0], odds, 1)]
    own = jnp.concatenate(parts, axis=1)
    odd = s % 2 == 1
    place = jnp.stack(
        [s * cols, jnp.int32(cols * space), m * tile, jnp.int32(rows), s % 2]
    ).astype(jnp.int32)
    if tm != 2:
        order = (m - jnp.arange(tm)) % tm
        w_first = jnp.take(w_first.reshape(3, 3, tm, acqs_own, channels), order, axis=2)
        w_first = w_first.reshape(3, 3, acqs, channels)
    w1, wr = pl.pallas_call(
        functools.partial(spread, tm == 2),
        out_shape=[
            jax.ShapeDtypeStruct((PAIR * channels, 3 * (PAIR + 2) * acqs), jnp.bfloat16),
            jax.ShapeDtypeStruct((LAYERS - 1, PAIR * channels, 3 * (PAIR + 2) * channels), jnp.bfloat16),
        ],
        in_specs=[smem, vmem, vmem],
        out_specs=[vmem, vmem],
        compiler_params=pltpu.CompilerParams(vmem_limit_bytes=8 * 1024 * 1024),
        cost_estimate=pl.CostEstimate(flops=100000000, bytes_accessed=1000000, transcendentals=0),
    )(place, w_first, w_rest)
    own, w1, wr = lax.optimization_barrier((own, w1, wr))
    mate = swapped(own, evens, 1)

    far = HALO - cols
    odd = s % 2 == 1

    def ends(x):
        edges = x[cols * wide :]
        head = jnp.concatenate([x[: far * wide], edges], axis=0)
        tail = jnp.concatenate([x[(cols - far) * wide : cols * wide], edges], axis=0)
        return head, tail

    head, tail = ends(own)
    ring = [(i, i - 2 if i else 1) for i in evens] + [(i + 1, i + 3 if i + 3 < space else i) for i in evens]
    across = lax.ppermute(jnp.where(odd, tail, head), "space", ring)
    head, tail = ends(mate)
    near = jnp.where(odd, tail, head)
    onward = parts[1:] + [near[:, d * acqs_own : (d + 1) * acqs_own] for d in range(tm)]
    counts = [x.shape[0] for x in onward]
    onward = swapped(jnp.concatenate(onward, axis=0), odds, 1)
    arrived, start = [], 0
    for count in counts:
        arrived.append(onward[start : start + count])
        start += count
    beside = jnp.concatenate(beside + arrived[: tm - 1], axis=1)
    extra = jnp.concatenate(arrived[tm - 1 :], axis=1)

    width = tile + LANES
    limit = pltpu.CompilerParams(vmem_limit_bytes=20 * 1024 * 1024)
    inputs = chip_layers(cols)
    depths = [acqs] + [channels] * (LAYERS - 1)
    reach = [2 * cols - 2 * RADIUS - 2 * n for n in range(inputs)]
    chip, *given = pl.pallas_call(
        chip_part,
        out_shape=[jax.ShapeDtypeStruct((2 * cols, acqs, width), jnp.float32)]
        + [jax.ShapeDtypeStruct((reach[n] * 3 * depths[n], width), jnp.bfloat16) for n in range(inputs)],
        in_specs=[smem] + [vmem] * 4,
        out_specs=[vmem] * (1 + inputs),
        compiler_params=limit,
        cost_estimate=pl.CostEstimate(flops=4000000000, bytes_accessed=4 * 10**6, transcendentals=10**6),
    )(place, own, mate, w1, wr)
    lacking = [cols + 2 * (LAYERS - n) - (reach[n] if n < inputs else 0) for n in range(LAYERS)]
    return pl.pallas_call(
        rest_part,
        out_shape=jax.ShapeDtypeStruct((channels, cols, tile), jnp.float32),
        in_specs=[smem] + [vmem] * (6 + inputs),
        out_specs=vmem,
        scratch_shapes=[
            pltpu.VMEM((2 * HALO - cols, acqs, width), jnp.float32),
            pltpu.VMEM((cols, channels, tile), jnp.float32),
        ]
        + [pltpu.VMEM((lacking[n] * 3 * depths[n], width), jnp.bfloat16) for n in range(LAYERS)],
        compiler_params=limit,
        cost_estimate=pl.CostEstimate(flops=2 * 10**9, bytes_accessed=4 * 10**6, transcendentals=10**6),
    )(place, beside, extra, across, w1, wr, chip, *given)


def solution(mesh):
    in_specs = (P("tm", "space", None), P(), P())
    out_specs = P(None, "space", "tm")
    return jax.shard_map(shards, mesh=mesh, in_specs=in_specs, out_specs=out_specs, check_vma=False)
```

```python
import functools

import jax
import jax.numpy as jnp
from jax import lax
from jax.experimental import pallas as pl
from jax.experimental.pallas import tpu as pltpu
from jax.sharding import PartitionSpec as P

LAYERS = 6
RADIUS = 3
HALO = RADIUS + LAYERS
MARGIN = 16
LANES = 128
PAIR = 2
BESIDE = 3


def swapped(x, lows, by):
    size, groups = lax.axis_size("space"), lax.axis_size("tm")
    partner = {i: i + by for i in lows} | {i + by: i for i in lows}
    alone = [i for i in range(size) if i not in partner]
    pairs = [(g * size + i, g * size + j) for g in range(groups) for i, j in partner.items()]
    if groups % 2 == 0:
        pairs += [(g * size + i, (g ^ 1) * size + i) for g in range(groups) for i in alone]
    else:
        pairs += [
            (g * size + i, g * size + j) for g in range(groups) for i, j in zip(alone, reversed(alone))
        ]
    return lax.ppermute(x, ("tm", "space"), pairs)


def rolled(x, by):
    return pltpu.roll(x, by % x.shape[-1], x.ndim - 1)


def pack(place, source, w_first, w_rest, first, rest, *refs):
    *outs, inten, sems = refs
    copies = [(source, inten), (w_first, first), (w_rest, rest)]
    copies = [pltpu.make_async_copy(x, y, sems.at[k]) for k, (x, y) in enumerate(copies)]
    for copy in copies:
        copy.start()
    acqs, cols, rows = inten.shape
    tiles, blocks = len(outs), outs[0].shape[0]
    copies[0].wait()
    tile = rows // tiles
    wide = tile // LANES
    sides = blocks - cols * wide
    lane = lax.broadcasted_iota(jnp.int32, (1, LANES), 1)
    slot = lane // MARGIN
    for d, out in enumerate(outs):
        t = place[0] + d
        t = jnp.where(t >= tiles, t - tiles, t)
        start = t * tile
        after = jnp.minimum(start + tile, rows - LANES)
        before = jnp.maximum(start - LANES, 0)
        right = jnp.zeros((acqs, LANES), jnp.float32)
        left = right
        for c in range(cols):
            main = jnp.log(inten[:, c, pl.ds(pl.multiple_of(start, LANES), tile)])
            for k in range(wide):
                out[c * wide + k] = main[:, k * LANES : (k + 1) * LANES].astype(jnp.bfloat16)
            if sides == 1:
                near = pl.multiple_of(jnp.where(t == 0, after, before), LANES)
                edge = jnp.log(inten[:, c, pl.ds(near, LANES)])
                edge = jnp.where(t == 0, rolled(edge, c * MARGIN), rolled(edge, (c + 1) * MARGIN))
                right = jnp.where(slot == c, edge, right)
            else:
                edge = jnp.log(inten[:, c, pl.ds(pl.multiple_of(after, LANES), LANES)])
                right = jnp.where(slot == c, rolled(edge, c * MARGIN), right)
                edge = jnp.log(inten[:, c, pl.ds(pl.multiple_of(before, LANES), LANES)])
                left = jnp.where(slot == c, rolled(edge, (c + 1) * MARGIN), left)
        out[cols * wide] = right.astype(jnp.bfloat16)
        if sides == 2:
            out[cols * wide + 1] = left.astype(jnp.bfloat16)
    for copy in copies[1:]:
        copy.wait()


def spread(swap, place, w_first, w_rest, first, rest):
    depth, channels = w_first.shape[2:]

    def laid(pieces):
        step = 3 * pieces[0].shape[1]
        rows = []
        for p in range(PAIR):
            before = [jnp.zeros((channels, p * step), jnp.float32)] if p else []
            after = [jnp.zeros((channels, (PAIR - 1 - p) * step), jnp.float32)] if p < PAIR - 1 else []
            rows.append(jnp.concatenate(before + pieces + after, axis=1))
        return jnp.concatenate(rows, axis=0).astype(jnp.bfloat16)

    odd = place[4] == 1
    taps = [(a, b) for a in range(3) for b in range(3)]
    late = [(jnp.where(odd, 2 - a, a), b) for a, b in taps]
    pieces = [w_first[a, b].astype(jnp.float32).T for a, b in late]
    if swap:
        half = depth // 2
        moved = [jnp.concatenate([x[:, half:], x[:, :half]], axis=1) for x in pieces]
        pieces = [jnp.where(place[2] == 0, x, y) for x, y in zip(pieces, moved)]
    first[...] = laid(pieces)
    for layer in range(LAYERS - 1):
        rest[layer] = laid([w_rest[layer, a, b].astype(jnp.float32) for a, b in late])


class Window:
    def __init__(self, place, cols, tile, acqs):
        self.cols, self.tile, self.acqs = cols, tile, acqs
        self.width = width = tile + LANES
        self.first, self.all_cols = place[0], place[1]
        self.base, self.all_rows = place[2], place[3]
        self.odd = place[4] == 1
        lane = lax.broadcasted_iota(jnp.int32, (1, width), 1)
        row = jnp.where(lane < tile + LANES // 2, lane, lane - width)
        inside = (row >= -MARGIN) & (row < tile + MARGIN)
        self.row = row + self.base
        self.inside = inside & (self.row >= 0) & (self.row < self.all_rows)
        self.row_mask = self.inside.astype(jnp.float32)
        count = jnp.minimum(self.row + RADIUS, self.all_rows - 1) - jnp.maximum(self.row - RADIUS, 0) + 1
        self.row_count = jnp.maximum(count, 1).astype(jnp.float32)

    def place_of(self, u):
        return self.first + jnp.where(self.odd, self.cols + HALO - 1 - u, u - HALO)

    def within(self, u):
        g = self.place_of(u)
        return (g >= 0) & (g < self.all_cols)

    def intensity(self, ref, k, slot, count, known):
        wide = self.tile // LANES
        k = jnp.where(self.odd, count - 1 - k, k)
        slot = jnp.where(self.odd, self.cols - 1 - slot, slot)
        parts = [ref[k * wide + n].astype(jnp.float32) for n in range(wide)]
        to_right = (self.cols - slot) * MARGIN % LANES
        to_left = (self.cols - slot - 1) * MARGIN % LANES
        edge = ref[count * wide].astype(jnp.float32)
        if ref.shape[0] == count * wide + 1:
            edge = pltpu.roll(edge, jnp.where(self.base == 0, to_right, to_left), 1)
        else:
            early = lax.broadcasted_iota(jnp.int32, (1, LANES), 1) < LANES // 2
            before = pltpu.roll(ref[count * wide + 1].astype(jnp.float32), to_left, 1)
            edge = jnp.where(early, pltpu.roll(edge, to_right, 1), before)
        coded = jnp.concatenate(parts + [edge], axis=1)
        ok = self.inside if known is None else self.inside & self.within(known)
        return jnp.where(ok, jnp.exp(coded), 0.0)

    def feature(self, u, inten):
        total = inten(u - RADIUS)
        for k in range(1 - RADIUS, RADIUS + 1):
            total = total + inten(u + k)
        three = rolled(total, 1) + total + rolled(total, -1)
        box = rolled(three, 2) + total + rolled(three, -2)
        g = self.place_of(u)
        count = jnp.minimum(g + RADIUS, self.all_cols - 1) - jnp.maximum(g - RADIUS, 0) + 1
        count = jnp.maximum(count, 1).astype(jnp.float32)
        local_mean = box * (1.0 / (self.row_count * count))
        ratio = jnp.sum(inten(u) / local_mean, axis=0, keepdims=True)
        feature = jnp.log(local_mean) + jnp.log(ratio / self.acqs)
        return jnp.where(self.inside & self.within(u), feature, 0.0).astype(jnp.bfloat16)

    def hidden(self, u, summed):
        ok = self.within(u).astype(jnp.float32)
        return (jnp.maximum(summed, 0.0) * (self.row_mask * ok)).astype(jnp.bfloat16)


def put(ref, k, value):
    depth = value.shape[0]
    to = k * 3 * depth
    ref[to : to + depth, :] = rolled(value, 1)
    ref[to + depth : to + 2 * depth, :] = value
    ref[to + 2 * depth : to + 3 * depth, :] = rolled(value, -1)


def columns(weight, wanted, source, channels, span, done):
    groups, at = [], 0
    while at < len(wanted):
        size = PAIR if wanted[at : at + PAIR] == list(range(wanted[at], wanted[at] + PAIR)) else 1
        groups.append((size, wanted[at]))
        at += size
    for size in (PAIR, 1):
        firsts = [j for n, j in groups if n == size]
        for start in range(0, len(firsts), BESIDE):
            some = firsts[start : start + BESIDE]
            taps = [jnp.concatenate([source(j + k, span) for k in range(size + 2)], axis=0) for j in some]
            used = weight if size == PAIR else weight[:channels, : taps[0].shape[0]]
            summed = jnp.dot(used, jnp.concatenate(taps, axis=1), preferred_element_type=jnp.float32)
            for n, j in enumerate(some):
                for p in range(size):
                    done(j + p, summed[p * channels : (p + 1) * channels, n * span : (n + 1) * span])


def chip_part(place, own, mate, w1, wr, inten, *layers):
    acqs, width = inten.shape[1:]
    cols = inten.shape[0] // 2
    tile = width - LANES
    channels = wr.shape[1] // PAIR
    win = Window(place, cols, tile, acqs)
    for k in range(cols):
        inten[k] = win.intensity(own, k, k, cols, None)
        inten[cols + k] = win.intensity(mate, k, k, cols, None)
    known = 2 * cols
    features = known - 2 * RADIUS
    for k in range(features):
        put(layers[0], k, win.feature(HALO + RADIUS + k, lambda u: inten[u - HALO]))
    for layer in range(len(layers) - 1):
        left = features - 2 * (layer + 1)
        depth = acqs if layer == 0 else channels

        def source(j, span, ref=layers[layer], depth=depth):
            return ref[j * 3 * depth : (j + 1) * 3 * depth, :span]

        def done(j, summed, layer=layer):
            put(layers[layer + 1], j, win.hidden(HALO + RADIUS + layer + 1 + j, summed))

        weight = w1[...] if layer == 0 else wr[layer - 1]
        columns(weight, list(range(left)), source, channels, width, done)


def rest_part(place, next_to, extra, across, w1, wr, chip, *refs):
    acqs, width = chip.shape[1:]
    count = chip_layers(chip.shape[0] // 2)
    given, out, inten, mine = refs[:count], refs[count], refs[count + 1], refs[count + 2 :]
    channels, cols, tile = out.shape
    win = Window(place, cols, tile, acqs)
    more = HALO - cols
    for k in range(more):
        inten[k] = win.intensity(extra, k, cols - more + k, more, k)
        inten[HALO + k] = win.intensity(across, k, k, more, HALO + 2 * cols + k)
    for k in range(cols):
        inten[more + k] = win.intensity(next_to, k, k, cols, more + k)

    def intensity(u):
        if HALO <= u < HALO + 2 * cols:
            return chip[u - HALO]
        return inten[u if u < HALO else u - 2 * cols]

    first = HALO
    for layer in range(LAYERS + 1):
        total = cols + 2 * (LAYERS - layer)
        have = max(2 * cols - 2 * RADIUS - 2 * layer, 0) if layer < count else 0
        wanted = [j for j in range(total) if not first <= j < first + have]
        if layer == 0:
            for k, f in enumerate(wanted):
                put(mine[0], k, win.feature(RADIUS + f, intensity))
        else:
            weight = w1[...] if layer == 1 else wr[layer - 2]

            def done(j, summed, layer=layer, wanted=wanted):
                if layer < LAYERS:
                    put(mine[layer], wanted.index(j), win.hidden(RADIUS + layer + j, summed))
                else:
                    out[:, pl.ds(jnp.where(win.odd, cols - 1 - j, j), 1), :] = summed[:, None, :]

            columns(weight, wanted, source, channels, tile if layer == LAYERS else width, done)
        depth = acqs if layer == 0 else channels

        def source(j, span, layer=layer, depth=depth, wanted=wanted):
            if j in wanted:
                ref, k = mine[layer], wanted.index(j)
            else:
                ref, k = given[layer], j - first
            return ref[k * 3 * depth : (k + 1) * 3 * depth, :span]


def chip_layers(cols):
    return min(LAYERS, cols - RADIUS)


def shards(intensity, w_first, w_rest):
    acqs_own, cols, rows = intensity.shape
    tm = lax.axis_size("tm")
    space = lax.axis_size("space")
    m = lax.axis_index("tm")
    s = lax.axis_index("space")
    tile = rows // tm
    wide = tile // LANES
    channels, acqs = w_first.shape[2:]
    vmem = pl.BlockSpec(memory_space=pltpu.VMEM)
    smem = pl.BlockSpec(memory_space=pltpu.SMEM)

    blocks = cols * wide + (1 if tm == 2 else 2)
    far_away = pl.BlockSpec(memory_space=pltpu.HBM)
    given = [intensity, w_first.transpose(0, 1, 3, 2), w_rest]
    w_first, w_rest, *packed = pl.pallas_call(
        pack,
        out_shape=[jax.ShapeDtypeStruct(x.shape, x.dtype) for x in given[1:]]
        + [jax.ShapeDtypeStruct((blocks, acqs_own, LANES), jnp.bfloat16)] * tm,
        in_specs=[smem] + [far_away] * 3,
        out_specs=[vmem] * (2 + tm),
        scratch_shapes=[pltpu.VMEM(intensity.shape, intensity.dtype), pltpu.SemaphoreType.DMA((3,))],
        compiler_params=pltpu.CompilerParams(vmem_limit_bytes=8 * 1024 * 1024),
    )(
        jnp.reshape(m, (1,)).astype(jnp.int32),
        *(pltpu.with_memory_space_constraint(x, pltpu.HBM) for x in given),
    )
    parts = [packed[0]]
    for d in range(1, tm):
        parts.append(lax.ppermute(packed[d], "tm", [(i, (i + d) % tm) for i in range(tm)]))
    evens = list(range(0, space, 2))
    odds = [i - 1 for i in evens[1:]]
    beside = [swapped(packed[0], odds, 1)]
    own = jnp.concatenate(parts, axis=1)
    odd = s % 2 == 1
    place = jnp.stack(
        [s * cols, jnp.int32(cols * space), m * tile, jnp.int32(rows), s % 2]
    ).astype(jnp.int32)
    if tm != 2:
        order = (m - jnp.arange(tm)) % tm
        w_first = jnp.take(w_first.reshape(3, 3, tm, acqs_own, channels), order, axis=2)
        w_first = w_first.reshape(3, 3, acqs, channels)
    w1, wr = pl.pallas_call(
        functools.partial(spread, tm == 2),
        out_shape=[
            jax.ShapeDtypeStruct((PAIR * channels, 3 * (PAIR + 2) * acqs), jnp.bfloat16),
            jax.ShapeDtypeStruct((LAYERS - 1, PAIR * channels, 3 * (PAIR + 2) * channels), jnp.bfloat16),
        ],
        in_specs=[smem, vmem, vmem],
        out_specs=[vmem, vmem],
        compiler_params=pltpu.CompilerParams(vmem_limit_bytes=8 * 1024 * 1024),
        cost_estimate=pl.CostEstimate(flops=100000000, bytes_accessed=1000000, transcendentals=0),
    )(place, w_first, w_rest)
    own, w1, wr = lax.optimization_barrier((own, w1, wr))
    mate = swapped(own, evens, 1)

    far = HALO - cols
    odd = s % 2 == 1

    def ends(x):
        edges = x[cols * wide :]
        head = jnp.concatenate([x[: far * wide], edges], axis=0)
        tail = jnp.concatenate([x[(cols - far) * wide : cols * wide], edges], axis=0)
        return head, tail

    head, tail = ends(own)
    ring = [(i, i - 2 if i else 1) for i in evens] + [(i + 1, i + 3 if i + 3 < space else i) for i in evens]
    across = lax.ppermute(jnp.where(odd, tail, head), "space", ring)
    head, tail = ends(mate)
    near = jnp.where(odd, tail, head)
    onward = parts[1:] + [near[:, d * acqs_own : (d + 1) * acqs_own] for d in range(tm)]
    counts = [x.shape[0] for x in onward]
    onward = swapped(jnp.concatenate(onward, axis=0), odds, 1)
    arrived, start = [], 0
    for count in counts:
        arrived.append(onward[start : start + count])
        start += count
    beside = jnp.concatenate(beside + arrived[: tm - 1], axis=1)
    extra = jnp.concatenate(arrived[tm - 1 :], axis=1)

    width = tile + LANES
    limit = pltpu.CompilerParams(vmem_limit_bytes=20 * 1024 * 1024)
    inputs = chip_layers(cols)
    depths = [acqs] + [channels] * (LAYERS - 1)
    reach = [2 * cols - 2 * RADIUS - 2 * n for n in range(inputs)]
    chip, *given = pl.pallas_call(
        chip_part,
        out_shape=[jax.ShapeDtypeStruct((2 * cols, acqs, width), jnp.float32)]
        + [jax.ShapeDtypeStruct((reach[n] * 3 * depths[n], width), jnp.bfloat16) for n in range(inputs)],
        in_specs=[smem] + [vmem] * 4,
        out_specs=[vmem] * (1 + inputs),
        compiler_params=limit,
        cost_estimate=pl.CostEstimate(flops=4000000000, bytes_accessed=4 * 10**6, transcendentals=10**6),
    )(place, own, mate, w1, wr)
    lacking = [cols + 2 * (LAYERS - n) - (reach[n] if n < inputs else 0) for n in range(LAYERS)]
    return pl.pallas_call(
        rest_part,
        out_shape=jax.ShapeDtypeStruct((channels, cols, tile), jnp.float32),
        in_specs=[smem] + [vmem] * (6 + inputs),
        out_specs=vmem,
        scratch_shapes=[
            pltpu.VMEM((2 * HALO - cols, acqs, width), jnp.float32),
        ]
        + [pltpu.VMEM((lacking[n] * 3 * depths[n], width), jnp.bfloat16) for n in range(LAYERS)],
        compiler_params=limit,
        cost_estimate=pl.CostEstimate(flops=2 * 10**9, bytes_accessed=4 * 10**6, transcendentals=10**6),
    )(place, beside, extra, across, w1, wr, chip, *given)


def solution(mesh):
    in_specs = (P("tm", "space", None), P(), P())
    out_specs = P(None, "space", "tm")
    return jax.shard_map(shards, mesh=mesh, in_specs=in_specs, out_specs=out_specs, check_vma=False)
```

```python
import functools

import jax
import jax.numpy as jnp
from jax import lax
from jax.experimental import pallas as pl
from jax.experimental.pallas import tpu as pltpu
from jax.sharding import PartitionSpec as P

LAYERS = 6
RADIUS = 3
HALO = RADIUS + LAYERS
MARGIN = 16
LANES = 128
PAIR = 2
BESIDE = 3


def swapped(x, lows, by):
    size, groups = lax.axis_size("space"), lax.axis_size("tm")
    partner = {i: i + by for i in lows} | {i + by: i for i in lows}
    alone = [i for i in range(size) if i not in partner]
    pairs = [(g * size + i, g * size + j) for g in range(groups) for i, j in partner.items()]
    if groups % 2 == 0:
        pairs += [(g * size + i, (g ^ 1) * size + i) for g in range(groups) for i in alone]
    else:
        pairs += [
            (g * size + i, g * size + j) for g in range(groups) for i, j in zip(alone, reversed(alone))
        ]
    return lax.ppermute(x, ("tm", "space"), pairs)


def rolled(x, by):
    return pltpu.roll(x, by % x.shape[-1], x.ndim - 1)


def pack(place, source, w_first, w_rest, first, rest, *refs):
    *outs, inten, sems = refs
    copies = [(source, inten), (w_first, first), (w_rest, rest)]
    copies = [pltpu.make_async_copy(x, y, sems.at[k]) for k, (x, y) in enumerate(copies)]
    for copy in copies:
        copy.start()
    acqs, cols, rows = inten.shape
    tiles, blocks = len(outs), outs[0].shape[0]
    copies[0].wait()
    tile = rows // tiles
    wide = tile // LANES
    sides = blocks - cols * wide
    lane = lax.broadcasted_iota(jnp.int32, (1, LANES), 1)
    slot = lane // MARGIN
    for d, out in enumerate(outs):
        t = place[0] + d
        t = jnp.where(t >= tiles, t - tiles, t)
        start = t * tile
        after = jnp.minimum(start + tile, rows - LANES)
        before = jnp.maximum(start - LANES, 0)
        right = jnp.zeros((acqs, LANES), jnp.float32)
        left = right
        for c in range(cols):
            main = jnp.log(inten[:, c, pl.ds(pl.multiple_of(start, LANES), tile)])
            for k in range(wide):
                out[c * wide + k] = main[:, k * LANES : (k + 1) * LANES].astype(jnp.bfloat16)
            if sides == 1:
                near = pl.multiple_of(jnp.where(t == 0, after, before), LANES)
                edge = jnp.log(inten[:, c, pl.ds(near, LANES)])
                edge = jnp.where(t == 0, rolled(edge, c * MARGIN), rolled(edge, (c + 1) * MARGIN))
                right = jnp.where(slot == c, edge, right)
            else:
                edge = jnp.log(inten[:, c, pl.ds(pl.multiple_of(after, LANES), LANES)])
                right = jnp.where(slot == c, rolled(edge, c * MARGIN), right)
                edge = jnp.log(inten[:, c, pl.ds(pl.multiple_of(before, LANES), LANES)])
                left = jnp.where(slot == c, rolled(edge, (c + 1) * MARGIN), left)
        out[cols * wide] = right.astype(jnp.bfloat16)
        if sides == 2:
            out[cols * wide + 1] = left.astype(jnp.bfloat16)
    for copy in copies[1:]:
        copy.wait()


def spread(swap, place, w_first, w_rest, first, rest):
    depth, channels = w_first.shape[2:]

    def laid(pieces):
        step = 3 * pieces[0].shape[1]
        rows = []
        for p in range(PAIR):
            before = [jnp.zeros((channels, p * step), jnp.float32)] if p else []
            after = [jnp.zeros((channels, (PAIR - 1 - p) * step), jnp.float32)] if p < PAIR - 1 else []
            rows.append(jnp.concatenate(before + pieces + after, axis=1))
        return jnp.concatenate(rows, axis=0).astype(jnp.bfloat16)

    odd = place[4] == 1
    taps = [(a, b) for a in range(3) for b in range(3)]
    late = [(jnp.where(odd, 2 - a, a), b) for a, b in taps]
    pieces = [w_first[a, b].astype(jnp.float32).T for a, b in late]
    if swap:
        half = depth // 2
        moved = [jnp.concatenate([x[:, half:], x[:, :half]], axis=1) for x in pieces]
        pieces = [jnp.where(place[2] == 0, x, y) for x, y in zip(pieces, moved)]
    first[...] = laid(pieces)
    for layer in range(LAYERS - 1):
        rest[layer] = laid([w_rest[layer, a, b].astype(jnp.float32) for a, b in late])


class Window:
    def __init__(self, place, cols, tile, acqs):
        self.cols, self.tile, self.acqs = cols, tile, acqs
        self.width = width = tile + LANES
        self.first, self.all_cols = place[0], place[1]
        self.base, self.all_rows = place[2], place[3]
        self.odd = place[4] == 1
        lane = lax.broadcasted_iota(jnp.int32, (1, width), 1)
        row = jnp.where(lane < tile + LANES // 2, lane, lane - width)
        inside = (row >= -MARGIN) & (row < tile + MARGIN)
        self.row = row + self.base
        self.inside = inside & (self.row >= 0) & (self.row < self.all_rows)
        self.row_mask = self.inside.astype(jnp.float32)
        count = jnp.minimum(self.row + RADIUS, self.all_rows - 1) - jnp.maximum(self.row - RADIUS, 0) + 1
        self.row_count = jnp.maximum(count, 1).astype(jnp.float32)

    def place_of(self, u):
        return self.first + jnp.where(self.odd, self.cols + HALO - 1 - u, u - HALO)

    def within(self, u):
        g = self.place_of(u)
        return (g >= 0) & (g < self.all_cols)

    def intensity(self, ref, k, slot, count, known):
        wide = self.tile // LANES
        k = jnp.where(self.odd, count - 1 - k, k)
        slot = jnp.where(self.odd, self.cols - 1 - slot, slot)
        parts = [ref[k * wide + n].astype(jnp.float32) for n in range(wide)]
        to_right = (self.cols - slot) * MARGIN % LANES
        to_left = (self.cols - slot - 1) * MARGIN % LANES
        edge = ref[count * wide].astype(jnp.float32)
        if ref.shape[0] == count * wide + 1:
            edge = pltpu.roll(edge, jnp.where(self.base == 0, to_right, to_left), 1)
        else:
            early = lax.broadcasted_iota(jnp.int32, (1, LANES), 1) < LANES // 2
            before = pltpu.roll(ref[count * wide + 1].astype(jnp.float32), to_left, 1)
            edge = jnp.where(early, pltpu.roll(edge, to_right, 1), before)
        coded = jnp.concatenate(parts + [edge], axis=1)
        ok = self.inside if known is None else self.inside & self.within(known)
        return jnp.where(ok, jnp.exp(coded), 0.0)

    def feature(self, u, inten):
        total = inten(u - RADIUS)
        for k in range(1 - RADIUS, RADIUS + 1):
            total = total + inten(u + k)
        three = rolled(total, 1) + total + rolled(total, -1)
        box = rolled(three, 2) + total + rolled(three, -2)
        g = self.place_of(u)
        count = jnp.minimum(g + RADIUS, self.all_cols - 1) - jnp.maximum(g - RADIUS, 0) + 1
        count = jnp.maximum(count, 1).astype(jnp.float32)
        local_mean = box * (1.0 / (self.row_count * count))
        ratio = jnp.sum(inten(u) / local_mean, axis=0, keepdims=True)
        feature = jnp.log(local_mean) + jnp.log(ratio / self.acqs)
        return jnp.where(self.inside & self.within(u), feature, 0.0).astype(jnp.bfloat16)

    def hidden(self, u, summed):
        ok = self.within(u).astype(jnp.float32)
        return (jnp.maximum(summed, 0.0) * (self.row_mask * ok)).astype(jnp.bfloat16)


def put(ref, k, value):
    depth = value.shape[0]
    to = k * 3 * depth
    ref[to : to + depth, :] = rolled(value, 1)
    ref[to + depth : to + 2 * depth, :] = value
    ref[to + 2 * depth : to + 3 * depth, :] = rolled(value, -1)


def columns(weight, wanted, source, channels, span, done):
    groups, at = [], 0
    while at < len(wanted):
        size = PAIR if wanted[at : at + PAIR] == list(range(wanted[at], wanted[at] + PAIR)) else 1
        groups.append((size, wanted[at]))
        at += size
    for size in (PAIR, 1):
        firsts = [j for n, j in groups if n == size]
        for start in range(0, len(firsts), BESIDE):
            some = firsts[start : start + BESIDE]
            taps = [jnp.concatenate([source(j + k, span) for k in range(size + 2)], axis=0) for j in some]
            used = weight if size == PAIR else weight[:channels, : taps[0].shape[0]]
            summed = jnp.dot(used, jnp.concatenate(taps, axis=1), preferred_element_type=jnp.float32)
            for n, j in enumerate(some):
                for p in range(size):
                    done(j + p, summed[p * channels : (p + 1) * channels, n * span : (n + 1) * span])


def chip_part(place, own, mate, w1, wr, inten, *layers):
    acqs, width = inten.shape[1:]
    cols = inten.shape[0] // 2
    tile = width - LANES
    channels = wr.shape[1] // PAIR
    win = Window(place, cols, tile, acqs)
    for k in range(cols):
        inten[k] = win.intensity(own, k, k, cols, None)
        inten[cols + k] = win.intensity(mate, k, k, cols, None)
    known = 2 * cols
    features = known - 2 * RADIUS
    for k in range(features):
        put(layers[0], k, win.feature(HALO + RADIUS + k, lambda u: inten[u - HALO]))
    for layer in range(len(layers) - 1):
        left = features - 2 * (layer + 1)
        depth = acqs if layer == 0 else channels

        def source(j, span, ref=layers[layer], depth=depth):
            return ref[j * 3 * depth : (j + 1) * 3 * depth, :span]

        def done(j, summed, layer=layer):
            put(layers[layer + 1], j, win.hidden(HALO + RADIUS + layer + 1 + j, summed))

        weight = w1[...] if layer == 0 else wr[layer - 1]
        columns(weight, list(range(left)), source, channels, width, done)


class Joined:
    def __init__(self, blocks, first, others, start, count):
        self.shape, self.first, self.others = (blocks,), first, others
        self.starts = [start + d * blocks for d in range(count)]

    def __getitem__(self, k):
        parts = [] if self.first is None else [self.first[k]]
        parts += [self.others[start + k] for start in self.starts]
        return jnp.concatenate([x.astype(jnp.float32) for x in parts], axis=0)


def rest_part(place, first_part, others, across, w1, wr, chip, *refs):
    acqs, width = chip.shape[1:]
    count = chip_layers(chip.shape[0] // 2)
    given, out, inten, mine = refs[:count], refs[count], refs[count + 1], refs[count + 2 :]
    channels, cols, tile = out.shape
    win = Window(place, cols, tile, acqs)
    more = HALO - cols
    blocks, tiles = first_part.shape[0], acqs // first_part.shape[1]
    next_to = Joined(blocks, first_part, others, 0, tiles - 1)
    extra = Joined(across.shape[0], None, others, (tiles - 1) * blocks, tiles)
    for k in range(more):
        inten[k] = win.intensity(extra, k, cols - more + k, more, k)
        inten[HALO + k] = win.intensity(across, k, k, more, HALO + 2 * cols + k)
    for k in range(cols):
        inten[more + k] = win.intensity(next_to, k, k, cols, more + k)

    def intensity(u):
        if HALO <= u < HALO + 2 * cols:
            return chip[u - HALO]
        return inten[u if u < HALO else u - 2 * cols]

    first = HALO
    for layer in range(LAYERS + 1):
        total = cols + 2 * (LAYERS - layer)
        have = max(2 * cols - 2 * RADIUS - 2 * layer, 0) if layer < count else 0
        wanted = [j for j in range(total) if not first <= j < first + have]
        if layer == 0:
            for k, f in enumerate(wanted):
                put(mine[0], k, win.feature(RADIUS + f, intensity))
        else:
            weight = w1[...] if layer == 1 else wr[layer - 2]

            def done(j, summed, layer=layer, wanted=wanted):
                if layer < LAYERS:
                    put(mine[layer], wanted.index(j), win.hidden(RADIUS + layer + j, summed))
                else:
                    out[:, pl.ds(jnp.where(win.odd, cols - 1 - j, j), 1), :] = summed[:, None, :]

            columns(weight, wanted, source, channels, tile if layer == LAYERS else width, done)
        depth = acqs if layer == 0 else channels

        def source(j, span, layer=layer, depth=depth, wanted=wanted):
            if j in wanted:
                ref, k = mine[layer], wanted.index(j)
            else:
                ref, k = given[layer], j - first
            return ref[k * 3 * depth : (k + 1) * 3 * depth, :span]


def chip_layers(cols):
    return min(LAYERS, cols - RADIUS)


def shards(intensity, w_first, w_rest):
    acqs_own, cols, rows = intensity.shape
    tm = lax.axis_size("tm")
    space = lax.axis_size("space")
    m = lax.axis_index("tm")
    s = lax.axis_index("space")
    tile = rows // tm
    wide = tile // LANES
    channels, acqs = w_first.shape[2:]
    vmem = pl.BlockSpec(memory_space=pltpu.VMEM)
    smem = pl.BlockSpec(memory_space=pltpu.SMEM)

    blocks = cols * wide + (1 if tm == 2 else 2)
    far_away = pl.BlockSpec(memory_space=pltpu.HBM)
    given = [intensity, w_first.transpose(0, 1, 3, 2), w_rest]
    w_first, w_rest, *packed = pl.pallas_call(
        pack,
        out_shape=[jax.ShapeDtypeStruct(x.shape, x.dtype) for x in given[1:]]
        + [jax.ShapeDtypeStruct((blocks, acqs_own, LANES), jnp.bfloat16)] * tm,
        in_specs=[smem] + [far_away] * 3,
        out_specs=[vmem] * (2 + tm),
        scratch_shapes=[pltpu.VMEM(intensity.shape, intensity.dtype), pltpu.SemaphoreType.DMA((3,))],
        compiler_params=pltpu.CompilerParams(vmem_limit_bytes=8 * 1024 * 1024),
    )(
        jnp.reshape(m, (1,)).astype(jnp.int32),
        *(pltpu.with_memory_space_constraint(x, pltpu.HBM) for x in given),
    )
    parts = [packed[0]]
    for d in range(1, tm):
        parts.append(lax.ppermute(packed[d], "tm", [(i, (i + d) % tm) for i in range(tm)]))
    evens = list(range(0, space, 2))
    odds = [i - 1 for i in evens[1:]]
    beside = [swapped(packed[0], odds, 1)]
    own = jnp.concatenate(parts, axis=1)
    odd = s % 2 == 1
    place = jnp.stack(
        [s * cols, jnp.int32(cols * space), m * tile, jnp.int32(rows), s % 2]
    ).astype(jnp.int32)
    if tm != 2:
        order = (m - jnp.arange(tm)) % tm
        w_first = jnp.take(w_first.reshape(3, 3, tm, acqs_own, channels), order, axis=2)
        w_first = w_first.reshape(3, 3, acqs, channels)
    w1, wr = pl.pallas_call(
        functools.partial(spread, tm == 2),
        out_shape=[
            jax.ShapeDtypeStruct((PAIR * channels, 3 * (PAIR + 2) * acqs), jnp.bfloat16),
            jax.ShapeDtypeStruct((LAYERS - 1, PAIR * channels, 3 * (PAIR + 2) * channels), jnp.bfloat16),
        ],
        in_specs=[smem, vmem, vmem],
        out_specs=[vmem, vmem],
        compiler_params=pltpu.CompilerParams(vmem_limit_bytes=8 * 1024 * 1024),
        cost_estimate=pl.CostEstimate(flops=100000000, bytes_accessed=1000000, transcendentals=0),
    )(place, w_first, w_rest)
    own, w1, wr = lax.optimization_barrier((own, w1, wr))
    mate = swapped(own, evens, 1)

    far = HALO - cols
    odd = s % 2 == 1

    def ends(x):
        edges = x[cols * wide :]
        head = jnp.concatenate([x[: far * wide], edges], axis=0)
        tail = jnp.concatenate([x[(cols - far) * wide : cols * wide], edges], axis=0)
        return head, tail

    head, tail = ends(own)
    ring = [(i, i - 2 if i else 1) for i in evens] + [(i + 1, i + 3 if i + 3 < space else i) for i in evens]
    across = lax.ppermute(jnp.where(odd, tail, head), "space", ring)
    head, tail = ends(mate)
    near = jnp.where(odd, tail, head)
    onward = parts[1:] + [near[:, d * acqs_own : (d + 1) * acqs_own] for d in range(tm)]
    onward = swapped(jnp.concatenate(onward, axis=0), odds, 1)

    width = tile + LANES
    limit = pltpu.CompilerParams(vmem_limit_bytes=20 * 1024 * 1024)
    inputs = chip_layers(cols)
    depths = [acqs] + [channels] * (LAYERS - 1)
    reach = [2 * cols - 2 * RADIUS - 2 * n for n in range(inputs)]
    chip, *given = pl.pallas_call(
        chip_part,
        out_shape=[jax.ShapeDtypeStruct((2 * cols, acqs, width), jnp.float32)]
        + [jax.ShapeDtypeStruct((reach[n] * 3 * depths[n], width), jnp.bfloat16) for n in range(inputs)],
        in_specs=[smem] + [vmem] * 4,
        out_specs=[vmem] * (1 + inputs),
        compiler_params=limit,
        cost_estimate=pl.CostEstimate(flops=4000000000, bytes_accessed=4 * 10**6, transcendentals=10**6),
    )(place, own, mate, w1, wr)
    lacking = [cols + 2 * (LAYERS - n) - (reach[n] if n < inputs else 0) for n in range(LAYERS)]
    return pl.pallas_call(
        rest_part,
        out_shape=jax.ShapeDtypeStruct((channels, cols, tile), jnp.float32),
        in_specs=[smem] + [vmem] * (6 + inputs),
        out_specs=vmem,
        scratch_shapes=[
            pltpu.VMEM((2 * HALO - cols, acqs, width), jnp.float32),
        ]
        + [pltpu.VMEM((lacking[n] * 3 * depths[n], width), jnp.bfloat16) for n in range(LAYERS)],
        compiler_params=limit,
        cost_estimate=pl.CostEstimate(flops=2 * 10**9, bytes_accessed=4 * 10**6, transcendentals=10**6),
    )(place, beside[0], onward, across, w1, wr, chip, *given)


def solution(mesh):
    in_specs = (P("tm", "space", None), P(), P())
    out_specs = P(None, "space", "tm")
    return jax.shard_map(shards, mesh=mesh, in_specs=in_specs, out_specs=out_specs, check_vma=False)
```
